32 devices in a mesh: fsdp: 2 (over y), replica: 16 (over z, x, core).
Axes of the slice: x: 2, y: 2, z: 4, core: 2. Of those that a mesh axis runs over, the one named last changes fastest.
Arguments:
- params: bfloat16 [16, 2, 2048, 512], P('replica', None, 'fsdp'), may hold values from -2.390625 to 2.390625
- momentum: bfloat16 [16, 2, 2048, 512], P('replica', None, 'fsdp'), may hold values from -6 to 6
- grads: bfloat16 [2, 16, 2, 2048, 512], P(None, 'replica', None, 'fsdp'), may hold values from -6 to 6
Outputs:
- new_params: bfloat16 [16, 2, 2048, 512], P('replica', None, 'fsdp')
- new_momentum: bfloat16 [16, 2, 2048, 512], P('replica', None, 'fsdp')
The draws below stay inside these ranges and needn't reach their ends.
All inputs are finite; a program needn't handle non-finite values.
Results may differ from the reference program's by a relative error of at most 0.013.
Values may be sent and summed in bfloat16 or wider, within the bound.
A program may use at most 128 MiB of HBM per device.

```python
import math
import jax
import jax.numpy as jnp
from jax import lax

ROWS = 2048
COLS = 512
NS_ITERS = 3
STEPS = 2
MATRICES = 2
REPLICAS = 16


def shard_levels(own_key, dims, shards, low, high):
    def one(position, blocks):
        draws = jax.random.uniform(jax.random.fold_in(jax.random.fold_in(own_key, 6), position), (blocks,), jnp.float32, low / len(shards), high / len(shards))
        return jnp.repeat(jnp.exp(draws), dims[position] // blocks).reshape((-1,) + (1,) * (len(dims) - position - 1))

    gain = one(*shards[0])
    for cut in shards[1:]:
        gain = gain * one(*cut)
    return gain


def normal_values(own_key, dims, width, limit, cuts=(), dtype=jnp.bfloat16):
    loudness = shard_levels(own_key, dims, cuts, -0.22, 0.18) if cuts else 1.0
    drawn = jax.random.normal(own_key, dims, jnp.float32) * width * loudness
    return jnp.minimum(jnp.maximum(drawn, -limit), limit).astype(dtype)


def setup_inputs(seed: int = 0) -> dict:
    splits = jax.random.split(jax.random.key(seed), 4)
    return {
        "params": normal_values(splits[0], (REPLICAS, MATRICES, ROWS, COLS), 0.3, 2.390625, ((0, 16), (2, 2))),
        "momentum": normal_values(splits[1], (REPLICAS, MATRICES, ROWS, COLS), 1.0, 6.0, ((0, 16), (2, 2))),
        "grads": normal_values(splits[2], (STEPS, REPLICAS, MATRICES, ROWS, COLS), 1.0, 6.0, ((1, 16), (3, 2))),
    }


BETA = 0.95
LEARN = 0.5
COEF_A = 3.4445
COEF_B = -4.775
COEF_C = 2.0315

def newton_schulz(matrix):
    xf = matrix.astype(jnp.float32)
    total = jnp.sqrt(jnp.sum(xf * xf))
    ycur = (xf / (total + 1e-07)).astype(jnp.bfloat16)
    for _ in range(NS_ITERS):
        gram = lax.dot_general(ycur, ycur, (((0,), (0,)), ((), ())), preferred_element_type=jnp.float32).astype(jnp.bfloat16)
        square = jnp.dot(gram, gram, preferred_element_type=jnp.float32)
        poly = (COEF_B * gram.astype(jnp.float32) + COEF_C * square).astype(jnp.bfloat16)
        ycur = (COEF_A * ycur.astype(jnp.float32) + jnp.dot(ycur, poly, preferred_element_type=jnp.float32)).astype(jnp.bfloat16)
    return ycur

def partner(values, span):
    shape = values.shape
    folded = values.reshape((shape[0] // (2 * span), 2, span) + shape[1:])
    return folded[:, ::-1].reshape(shape)

def reference(params, momentum, grads):
    step_scale = LEARN * 0.2 * math.sqrt(max(ROWS, COLS))
    pcur = params
    mcur = momentum
    for step in range(STEPS):
        grad = grads[step].astype(jnp.float32)
        m_new = (BETA * mcur.astype(jnp.float32) + grad).astype(jnp.bfloat16)
        nest = (grad + BETA * m_new.astype(jnp.float32)).astype(jnp.bfloat16)
        flat = nest.reshape(-1, ROWS, COLS)
        update = lax.map(newton_schulz, flat).reshape(nest.shape)
        local = (pcur.astype(jnp.float32) - step_scale * update.astype(jnp.float32)).astype(jnp.bfloat16)
        span = 2 ** step
        lfloat = local.astype(jnp.float32)
        pcur = (0.5 * (lfloat + partner(lfloat, span))).astype(jnp.bfloat16)
        mfloat = m_new.astype(jnp.float32)
        mcur = (0.5 * (mfloat + partner(mfloat, span))).astype(jnp.bfloat16)
    return (pcur, mcur)
```

```python
import functools
import math

import jax
import jax.numpy as jnp
from jax import lax
from jax.experimental import pallas as pl
from jax.experimental.pallas import tpu as pltpu
from jax.sharding import PartitionSpec as P

ROWS = 2048
COLS = 512
NS_ITERS = 3
STEPS = 2


BETA = 0.95
LEARN = 0.5
COEF_A = 3.4445
COEF_B = -4.775
COEF_C = 2.0315

MESH = pl.DeviceIdType.MESH
BF16 = jnp.bfloat16
F32 = jnp.float32


def partner(value, axis, apart):
    mask = 2**apart
    pairs = [(source, source ^ mask) for source in range(lax.axis_size(axis))]
    return lax.ppermute(value, axis, pairs)


def dot(a, b):
    return jnp.dot(a, b, preferred_element_type=F32)


def reduce_gram(nest):
    part = lax.dot_general(nest, nest, (((0,), (0,)), ((), ())), preferred_element_type=F32)
    half = part.shape[0] // 2
    packed = jnp.concatenate([part[:half], part[half:, half:]], axis=1).astype(BF16)
    if lax.axis_size("fsdp") == 2:
        whole = packed.astype(F32) + partner(packed, "fsdp", 0).astype(F32)
    else:
        whole = lax.psum(packed.astype(F32), "fsdp")
    top, low = whole[:, : 2 * half], whole[:, 2 * half :]
    return jnp.concatenate([top, jnp.concatenate([top[:, half:].T, low], axis=1)], axis=0)


def orthogonalize(nest, gram):
    scale = 1.0 / (jnp.sqrt(jnp.trace(gram)) + 1e-07)
    gram = gram * (scale * scale)
    ycur = (nest.astype(F32) * scale).astype(BF16)
    for it in range(NS_ITERS):
        low = gram.astype(BF16)
        poly = (COEF_B * low.astype(F32) + COEF_C * dot(low, low)).astype(BF16)
        if it < NS_ITERS - 1:
            right = COEF_A * gram + dot(low, poly)
            gram = COEF_A * right + dot(poly, right.astype(BF16))
        ycur = COEF_A * ycur.astype(F32) + dot(ycur, poly)
        if it < NS_ITERS - 1:
            ycur = ycur.astype(BF16)
    return ycur


def mean(a, b):
    return (0.5 * (a.astype(F32) + b.astype(F32))).astype(BF16)


def shards(params, momentum, grads):
    mats = params.shape[1]
    step_scale = LEARN * 0.2 * math.sqrt(max(ROWS, COLS))
    nests = []
    mcur = [momentum[0, i] for i in range(mats)]
    for step in range(STEPS):
        grad = [grads[step, 0, i].astype(F32) for i in range(mats)]
        m_new = [(BETA * m.astype(F32) + g).astype(BF16) for m, g in zip(mcur, grad)]
        nests.append([(g + BETA * m.astype(F32)).astype(BF16) for m, g in zip(m_new, grad)])
        mcur = [mean(m, partner(m, "replica", step)) for m in m_new]
    grams = [[reduce_gram(n) for n in row] for row in nests]
    pcur = [params[0, i] for i in range(mats)]
    for step in range(STEPS):
        for i in range(mats):
            update = orthogonalize(nests[step][i], grams[step][i])
            local = (pcur[i].astype(F32) - step_scale * update).astype(BF16)
            pcur[i] = mean(local, partner(local, "replica", step))
    return (jnp.stack(pcur)[None], jnp.stack(mcur)[None])


SUB = 64
SEG = 512
CHUNK = 256


def kernel(seg_rows, chunk, p_hbm, m_hbm, g_hbm, p_out, m_out,
           p, m, g, mn1, rm1, mn2, rm2, n, l1, rl1, l2, rl2,
           m1, m1b, p1, p1b, gb, gs, gr, gram, low, poly, right, rlow,
           isem, psem, msem, esem, lsem, usem, bsem, wsem, osem):
    mats, rows, cols = p.shape
    half = cols // 2
    share = rows // 2
    per = rows // chunk
    per_seg = rows // seg_rows
    segs = mats * per_seg
    spare = STEPS * mats
    step_scale = LEARN * 0.2 * math.sqrt(max(ROWS, COLS))
    side = lax.axis_index("fsdp")
    rep = lax.axis_index("replica")
    core = rep % 2
    across = {"fsdp": 1 - side}
    near = {"replica": rep + 1 - 2 * core}
    far = {"replica": rep + 2 - 4 * ((rep // 2) % 2)}
    mine = pl.ds(pl.multiple_of(core * share, share), share)
    others = pl.ds(1, mats - 1)

    def each(total, body):
        lax.fori_loop(0, total, lambda k, c: (body(k), c)[1], 0)

    def part(c):
        return pl.ds(pl.multiple_of(c * chunk, chunk), chunk)

    def place(seg):
        return seg // per_seg, pl.ds((seg % per_seg) * seg_rows, seg_rows)

    def pieces(start, size, body):
        each(size // SUB, lambda k: body(pl.ds(pl.multiple_of(start + k * SUB, SUB), SUB)))

    def mean(a, b):
        return (0.5 * (a.astype(F32) + b.astype(F32))).astype(BF16)

    def fetch(which, seg):
        i, r = place(seg)
        src, dst = {
            0: (m_hbm.at[0, i, r], m.at[i, r]),
            1: (g_hbm.at[0, 0, i, r], g.at[0, i, r]),
            2: (g_hbm.at[1, 0, i, r], g.at[1, i, r]),
        }[which]
        return pltpu.make_async_copy(src, dst, isem.at[which, seg])

    def fetch_params():
        return pltpu.make_async_copy(p_hbm.at[0], p, psem)

    def send(src, dst, sent, got, peer):
        return pltpu.make_async_remote_copy(
            src_ref=src, dst_ref=dst, send_sem=sent, recv_sem=got, device_id=peer, device_id_type=MESH)

    def raw():
        return send(g_hbm.at[1, 0, 0], gb, osem.at[0], wsem.at[0], far)

    def first(i, r, seg):
        return send(mn1.at[i, r], rm1.at[i, r], osem.at[1], msem.at[seg], near)

    def second(i, r):
        return send(mn2.at[i, r], rm2.at[i, r], osem.at[2], wsem.at[1], far)

    def share_m():
        return send(m1.at[mine], m1b.at[mine], osem.at[3], wsem.at[2], far)

    def pass_m():
        return send(m1b.at[mine], m1b.at[mine], osem.at[4], esem.at[0], near)

    def third(i, r):
        return send(l1.at[i, r], rl1.at[i, r], osem.at[5], lsem.at[i], near)

    def share_p():
        return send(p1.at[mine], p1b.at[mine], osem.at[6], wsem.at[3], far)

    def pass_p():
        return send(p1b.at[mine], p1b.at[mine], osem.at[7], esem.at[1], near)

    def fourth(i, r, at):
        return send(l2.at[i, r], rl2.at[i, r], osem.at[8], usem.at[at], far)

    def blocks(slot):
        return send(gs.at[slot], gr.at[slot], osem.at[9], bsem.at[slot], across)

    barrier = pltpu.get_barrier_semaphore()
    for peer in (far, near, across):
        pl.semaphore_signal(barrier, inc=1, device_id=peer, device_id_type=MESH)
    for which in range(3):
        fetch(which, 0).start()
    pl.semaphore_wait(barrier, 3)
    raw().start()
    for seg in range(1, segs):
        for which in range(3):
            fetch(which, seg).start()
    fetch_params().start()

    def momentum_one(seg):
        fetch(0, seg).wait()
        fetch(1, seg).wait()
        i, span = place(seg)

        def body(r):
            grad = g[0, i, r].astype(F32)
            new = (BETA * m[i, r].astype(F32) + grad).astype(BF16)
            mn1[i, r] = new
            n[i, r] = (grad + BETA * new.astype(F32)).astype(BF16)

        pieces(span.start, span.size, body)
        first(i, span, seg).start()

    def momentum_two(seg):
        fetch(2, seg).wait()
        i, span = place(seg)
        first(i, span, seg).wait_recv()

        def body(r):
            grad = g[1, i, r].astype(F32)
            cur = mean(mn1[i, r], rm1[i, r])
            if i == 0:
                m1[r] = cur
            new = (BETA * cur.astype(F32) + grad).astype(BF16)
            mn2[i, r] = new
            n[mats + i, r] = (grad + BETA * new.astype(F32)).astype(BF16)

        pieces(span.start, span.size, body)
        if i > 0:
            second(i, span).start()
        elif seg == per_seg - 1:
            share_m().start()

    for seg in range(segs + 1):
        if seg < segs:
            momentum_one(seg)
        if seg > 0:
            momentum_two(seg - 1)

    def gram_part(slot):
        left, low_part = n[slot, :, :half], n[slot, :, half:]
        dims = (((0,), (0,)), ((), ()))
        gs[slot, :, :cols] = lax.dot_general(left, n[slot], dims, preferred_element_type=F32).astype(BF16)
        gs[slot, :, cols:] = lax.dot_general(low_part, low_part, dims, preferred_element_type=F32).astype(BF16)
        blocks(slot).start()

    each(STEPS * mats, gram_part)
    fetch_params().wait()

    def polys(slot):
        blocks(slot).wait_recv()
        top = gs[slot, :, :cols].astype(F32) + gr[slot, :, :cols].astype(F32)
        end = gs[slot, :, cols:].astype(F32) + gr[slot, :, cols:].astype(F32)
        eye = lax.broadcasted_iota(jnp.int32, (half, half), 0) == lax.broadcasted_iota(jnp.int32, (half, half), 1)
        trace = jnp.sum(jnp.where(eye, top[:, :half] + end, 0.0), keepdims=True)
        scale = 1.0 / (jnp.sqrt(trace) + 1e-07)
        square = scale * scale
        gram[:half, :] = top * square
        gram[half:, half:] = end * square
        gram[half:, :half] = (top[:, half:] * square).T
        low[...] = gram[...].astype(BF16)
        for it in range(NS_ITERS):
            def make_poly(t):
                r = pl.ds(pl.multiple_of(t * half, half), half)
                poly[it, r] = (COEF_B * low[r].astype(F32) + COEF_C * dot(low[r], low[...])).astype(BF16)

            def make_right(t):
                r = pl.ds(pl.multiple_of(t * half, half), half)
                value = COEF_A * gram[r] + dot(low[r], poly[it])
                right[r] = value
                rlow[r] = value.astype(BF16)

            def make_gram(t):
                r = pl.ds(pl.multiple_of(t * half, half), half)
                value = COEF_A * right[r] + dot(poly[it, r], rlow[...])
                gram[r] = value
                low[r] = value.astype(BF16)

            each(2, make_poly)
            if it < NS_ITERS - 1:
                each(2, make_right)
                each(2, make_gram)
        return scale

    def update(slot, r, scale):
        ycur = (n[slot, r].astype(F32) * scale).astype(BF16)
        for it in range(NS_ITERS):
            ycur = COEF_A * ycur.astype(F32) + dot(ycur, poly[it])
            if it < NS_ITERS - 1:
                ycur = ycur.astype(BF16)
        return ycur

    def step_one(i):
        scale = polys(i)

        def body(c):
            r = part(c)
            l1[i, r] = (p[i, r].astype(F32) - step_scale * update(i, r, scale)).astype(BF16)
            third(i, r).start()

        each(per, body)

    each(mats, step_one)

    third(0, pl.ds(0, rows)).wait_recv()

    def pair_mean(r):
        p1[r] = mean(l1[0, r], rl1[0, r])

    pieces(0, rows, pair_mean)
    share_p().start()

    def step_two(i):
        scale = polys(mats + i)
        third(i, pl.ds(0, rows)).wait_recv()

        def body(c):
            r = part(c)
            cur = mean(l1[i, r], rl1[i, r]).astype(F32)
            l2[i, r] = (cur - step_scale * update(mats + i, r, scale)).astype(BF16)
            fourth(i, r, i * (1 - c // (per - 1)) if i == mats - 1 else i).start()

        each(per, body)

    for i in range(1, mats):
        step_two(i)

    share_m().wait_recv()
    pass_m().start()
    raw().wait_recv()
    pass_m().wait_recv()

    def momentum_far(r):
        grad = gb[r].astype(F32)
        new = (BETA * m1b[r].astype(F32) + grad).astype(BF16)
        n[spare, r] = (grad + BETA * new.astype(F32)).astype(BF16)
        m_out[0, 0, r] = mean(mn2[0, r], new)

    pieces(0, rows, momentum_far)
    gram_part(spare)

    own_scale = polys(mats)

    def own(c):
        r = part(c)
        l2[0, r] = (p1[r].astype(F32) - step_scale * update(mats, r, own_scale)).astype(BF16)

    each(per, own)

    far_scale = polys(spare)
    share_p().wait_recv()
    pass_p().start()
    pass_p().wait_recv()

    def theirs(c):
        r = part(c)
        local = (p1b[r].astype(F32) - step_scale * update(spare, r, far_scale)).astype(BF16)
        p_out[0, 0, r] = mean(l2[0, r], local)

    each(per, theirs)

    second(others, pl.ds(0, rows)).wait_recv()
    for i in range(1, mats):
        def momentum_out(r):
            m_out[0, i, r] = mean(mn2[i, r], rm2[i, r])

        pieces(0, rows, momentum_out)

    for seg in range(segs):
        first(*place(seg), seg).wait_send()
    for copy in (raw(), second(others, pl.ds(0, rows)), share_m(), pass_m(), share_p(), pass_p()):
        copy.wait_send()
    for i in range(mats):
        third(i, pl.ds(0, rows)).wait_send()
    each(STEPS * mats + 1, lambda slot: blocks(slot).wait_send())

    for i in range(1, mats):
        ends = [(0, rows - chunk, i), (rows - chunk, chunk, 0)] if i == mats - 1 else [(0, rows, i)]
        for start, size, at in ends:
            fourth(i, pl.ds(start, size), at).wait_recv()

            def params_out(r):
                p_out[0, i, r] = mean(l2[i, r], rl2[i, r])

            pieces(start, size, params_out)
    fourth(others, pl.ds(0, rows), 0).wait_send()


def put(p, m, p_out, m_out, sem):
    copies = [
        pltpu.make_async_copy(src.at[0, i], dst.at[0, i], sem.at[k, i])
        for k, (src, dst) in enumerate(((p, p_out), (m, m_out))) for i in range(p.shape[1])
    ]
    for copy in copies:
        copy.start()
    for copy in copies:
        copy.wait()


def fused(params, momentum, grads):
    _, mats, rows, cols = params.shape
    seg_rows, chunk = min(SEG, rows // 2), min(CHUNK, rows // 2)
    whole, one = pltpu.VMEM((mats, rows, cols), BF16), pltpu.VMEM((rows, cols), BF16)
    slots = STEPS * mats + 1
    pack = pltpu.VMEM((slots, cols // 2, cols + cols // 2), BF16)
    small, small_low = pltpu.VMEM((cols, cols), F32), pltpu.VMEM((cols, cols), BF16)
    dma = pltpu.SemaphoreType.DMA
    segs = mats * (rows // seg_rows)
    anywhere = pl.BlockSpec(memory_space=pl.ANY)
    results = pl.pallas_call(
        functools.partial(kernel, seg_rows, chunk),
        out_shape=[pltpu.VMEM(params.shape, BF16)] * 2,
        in_specs=[anywhere] * 3,
        out_specs=[pl.BlockSpec(memory_space=pltpu.VMEM)] * 2,
        scratch_shapes=[
            whole, whole, pltpu.VMEM((STEPS, mats, rows, cols), BF16),
            whole, whole, whole, whole, pltpu.VMEM((slots, rows, cols), BF16),
            whole, whole, whole, whole, one, one, one, one, one, pack, pack,
            small, small_low, pltpu.VMEM((NS_ITERS, cols, cols), BF16), small, small_low,
            dma((3, segs)), dma(()), dma((segs,)), dma((2,)), dma((mats,)), dma((mats,)), dma((slots,)), dma((4,)),
            dma((10,)),
        ],
        compiler_params=pltpu.CompilerParams(
            collective_id=0, has_side_effects=True, vmem_limit_bytes=59 * 2**20),
    )(params, momentum, grads)
    return pl.pallas_call(
        put,
        out_shape=[jax.ShapeDtypeStruct(params.shape, BF16)] * 2,
        in_specs=[pl.BlockSpec(memory_space=pltpu.VMEM)] * 2,
        out_specs=[anywhere] * 2,
        scratch_shapes=[dma((2, mats))],
        compiler_params=pltpu.CompilerParams(vmem_limit_bytes=2**20),
    )(*[pltpu.with_memory_space_constraint(r, pltpu.VMEM) for r in results])


def solution(mesh):
    def program(params, momentum, grads):
        paired = mesh.shape["fsdp"] == 2 and params.shape[1] > 1
        return (fused if paired else shards)(params, momentum, grads)

    return jax.shard_map(
        program,
        mesh=mesh,
        in_specs=(
            P("replica", None, "fsdp", None),
            P("replica", None, "fsdp", None),
            P(None, "replica", None, "fsdp", None),
        ),
        out_specs=(P("replica", None, "fsdp", None), P("replica", None, "fsdp", None)),
        check_vma=False,
    )
```

```python
import functools
import math

import jax
import jax.numpy as jnp
from jax import lax
from jax.experimental import pallas as pl
from jax.experimental.pallas import tpu as pltpu
from jax.sharding import PartitionSpec as P

ROWS = 2048
COLS = 512
NS_ITERS = 3
STEPS = 2


BETA = 0.95
LEARN = 0.5
COEF_A = 3.4445
COEF_B = -4.775
COEF_C = 2.0315

MESH = pl.DeviceIdType.MESH
BF16 = jnp.bfloat16
F32 = jnp.float32


def partner(value, axis, apart):
    mask = 2**apart
    pairs = [(source, source ^ mask) for source in range(lax.axis_size(axis))]
    return lax.ppermute(value, axis, pairs)


def dot(a, b):
    return jnp.dot(a, b, preferred_element_type=F32)


def reduce_gram(nest):
    part = lax.dot_general(nest, nest, (((0,), (0,)), ((), ())), preferred_element_type=F32)
    half = part.shape[0] // 2
    packed = jnp.concatenate([part[:half], part[half:, half:]], axis=1).astype(BF16)
    if lax.axis_size("fsdp") == 2:
        whole = packed.astype(F32) + partner(packed, "fsdp", 0).astype(F32)
    else:
        whole = lax.psum(packed.astype(F32), "fsdp")
    top, low = whole[:, : 2 * half], whole[:, 2 * half :]
    return jnp.concatenate([top, jnp.concatenate([top[:, half:].T, low], axis=1)], axis=0)


def orthogonalize(nest, gram):
    scale = 1.0 / (jnp.sqrt(jnp.trace(gram)) + 1e-07)
    gram = gram * (scale * scale)
    ycur = (nest.astype(F32) * scale).astype(BF16)
    for it in range(NS_ITERS):
        low = gram.astype(BF16)
        poly = (COEF_B * low.astype(F32) + COEF_C * dot(low, low)).astype(BF16)
        if it < NS_ITERS - 1:
            right = COEF_A * gram + dot(low, poly)
            gram = COEF_A * right + dot(poly, right.astype(BF16))
        ycur = COEF_A * ycur.astype(F32) + dot(ycur, poly)
        if it < NS_ITERS - 1:
            ycur = ycur.astype(BF16)
    return ycur


def mean(a, b):
    return (0.5 * (a.astype(F32) + b.astype(F32))).astype(BF16)


def shards(params, momentum, grads):
    mats = params.shape[1]
    step_scale = LEARN * 0.2 * math.sqrt(max(ROWS, COLS))
    nests = []
    mcur = [momentum[0, i] for i in range(mats)]
    for step in range(STEPS):
        grad = [grads[step, 0, i].astype(F32) for i in range(mats)]
        m_new = [(BETA * m.astype(F32) + g).astype(BF16) for m, g in zip(mcur, grad)]
        nests.append([(g + BETA * m.astype(F32)).astype(BF16) for m, g in zip(m_new, grad)])
        mcur = [mean(m, partner(m, "replica", step)) for m in m_new]
    grams = [[reduce_gram(n) for n in row] for row in nests]
    pcur = [params[0, i] for i in range(mats)]
    for step in range(STEPS):
        for i in range(mats):
            update = orthogonalize(nests[step][i], grams[step][i])
            local = (pcur[i].astype(F32) - step_scale * update).astype(BF16)
            pcur[i] = mean(local, partner(local, "replica", step))
    return (jnp.stack(pcur)[None], jnp.stack(mcur)[None])


SUB = 64
SEG = 512
HEAD = 128
CHUNK = 256


def kernel(seg_rows, chunk, p_hbm, m_hbm, g_hbm, p_out, m_out,
           p, m, g, mn1, rm1, mn2, rm2, n, l1, rl1, l2, rl2,
           m1, m1b, p1, p1b, gb, gs, gr, gram, low, poly, right, rlow,
           isem, psem, msem, esem, lsem, usem, bsem, wsem, osem, hsem):
    mats, rows, cols = p.shape
    half = cols // 2
    share = rows // 2
    per = rows // chunk
    per_seg = rows // seg_rows
    segs = mats * per_seg
    spare = STEPS * mats
    step_scale = LEARN * 0.2 * math.sqrt(max(ROWS, COLS))
    side = lax.axis_index("fsdp")
    rep = lax.axis_index("replica")
    core = rep % 2
    late = (rep // 2) % 2
    across = {"fsdp": 1 - side}
    near = {"replica": rep + 1 - 2 * core}
    far = {"replica": rep + 2 - 4 * late}
    mine = pl.ds(pl.multiple_of(core * share, share), share)
    others = pl.ds(1, mats - 1)

    def each(total, body):
        lax.fori_loop(0, total, lambda k, c: (body(k), c)[1], 0)

    def part(c):
        return pl.ds(pl.multiple_of(c * chunk, chunk), chunk)

    def place(seg):
        return seg // per_seg, pl.ds((seg % per_seg) * seg_rows, seg_rows)

    def pieces(start, size, body):
        each(size // SUB, lambda k: body(pl.ds(pl.multiple_of(start + k * SUB, SUB), SUB)))

    def mean(a, b):
        return (0.5 * (a.astype(F32) + b.astype(F32))).astype(BF16)

    def fetch(which, seg):
        i, r = place(seg)
        src, dst = {
            0: (m_hbm.at[0, i, r], m.at[i, r]),
            1: (g_hbm.at[0, 0, i, r], g.at[0, i, r]),
            2: (g_hbm.at[1, 0, i, r], g.at[1, i, r]),
        }[which]
        return pltpu.make_async_copy(src, dst, isem.at[which, seg])

    heads = [pl.ds(0, HEAD), pl.ds(HEAD, rows - HEAD)]

    def fetch_raw(k):
        return pltpu.make_async_copy(g_hbm.at[1, 0, 0, heads[k]], g.at[1, 0, heads[k]], isem.at[2, k])

    def fetch_params():
        return pltpu.make_async_copy(p_hbm.at[0], p, psem)

    def send(src, dst, sent, got, peer):
        return pltpu.make_async_remote_copy(
            src_ref=src, dst_ref=dst, send_sem=sent, recv_sem=got, device_id=peer, device_id_type=MESH)

    def raw(src, r):
        return send(src, gb.at[r], osem.at[0], wsem.at[0], far)

    def first(i, r, seg):
        return send(mn1.at[i, r], rm1.at[i, r], osem.at[1], msem.at[seg], near)

    def second(i, r):
        return send(mn2.at[i, r], rm2.at[i, r], osem.at[2], wsem.at[1], far)

    def share_m():
        return send(m1.at[mine], m1b.at[mine], osem.at[3], wsem.at[2], far)

    def pass_m():
        return send(m1b.at[mine], m1b.at[mine], osem.at[4], esem.at[0], near)

    def third(i, r):
        return send(l1.at[i, r], rl1.at[i, r], osem.at[5], lsem.at[i], near)

    def share_p():
        return send(p1.at[mine], p1b.at[mine], osem.at[6], wsem.at[3], far)

    def pass_p():
        return send(p1b.at[mine], p1b.at[mine], osem.at[7], esem.at[1], near)

    def fourth(i, r, at):
        return send(l2.at[i, r], rl2.at[i, r], osem.at[8], usem.at[at], far)

    def blocks(slot):
        return send(gs.at[slot], gr.at[slot], osem.at[9], bsem.at[slot], across)

    barrier = pltpu.get_barrier_semaphore()
    pl.semaphore_signal(barrier, inc=1, device_id=far, device_id_type=MESH)

    @pl.when(late == 0)
    def _():
        for peer in (near, across):
            pl.semaphore_signal(barrier, inc=1, device_id=peer, device_id_type=MESH)

    def fetch_rest():
        for seg in range(segs):
            for which in range(2 if seg < per_seg else 3):
                fetch(which, seg).start()
        fetch_params().start()

    @pl.when(late == 0)
    def _():
        for k in range(2):
            fetch_raw(k).start()
        fetch_rest()
        for k in range(2):
            fetch_raw(k).wait()
        pl.semaphore_wait(barrier, 3)
        for r in heads:
            raw(g.at[1, 0, r], r).start()
        for peer in (near, across):
            pl.semaphore_signal(hsem.at[0], inc=1, device_id=peer, device_id_type=MESH)

    @pl.when(late == 1)
    def _():
        pl.semaphore_wait(barrier, 1)
        raw(g_hbm.at[1, 0, 0, heads[0]], heads[0]).start()
        for k in (1, 0):
            fetch_raw(k).start()
        fetch_raw(1).wait()
        raw(g.at[1, 0, heads[1]], heads[1]).start()
        fetch_rest()
        fetch_raw(0).wait()

    def meet():
        @pl.when(late == 0)
        def _():
            pl.semaphore_wait(hsem.at[0], 2)
            pl.semaphore_signal(hsem.at[1], inc=1, device_id=far, device_id_type=MESH)

        @pl.when(late == 1)
        def _():
            pl.semaphore_wait(hsem.at[1], 1)

    def momentum_one(seg):
        fetch(0, seg).wait()
        fetch(1, seg).wait()
        i, span = place(seg)

        def body(r):
            grad = g[0, i, r].astype(F32)
            new = (BETA * m[i, r].astype(F32) + grad).astype(BF16)
            mn1[i, r] = new
            n[i, r] = (grad + BETA * new.astype(F32)).astype(BF16)

        pieces(span.start, span.size, body)
        if seg == 0:
            meet()
        first(i, span, seg).start()

    def momentum_two(seg):
        i, span = place(seg)
        if i > 0:
            fetch(2, seg).wait()
        first(i, span, seg).wait_recv()

        def body(r):
            grad = g[1, i, r].astype(F32)
            cur = mean(mn1[i, r], rm1[i, r])
            if i == 0:
                m1[r] = cur
            new = (BETA * cur.astype(F32) + grad).astype(BF16)
            mn2[i, r] = new
            n[mats + i, r] = (grad + BETA * new.astype(F32)).astype(BF16)

        pieces(span.start, span.size, body)
        if i > 0:
            second(i, span).start()
        elif seg == per_seg - 1:
            share_m().start()

    for seg in range(segs + 1):
        if seg < segs:
            momentum_one(seg)
        if seg > 0:
            momentum_two(seg - 1)

    def gram_part(slot):
        left, low_part = n[slot, :, :half], n[slot, :, half:]
        dims = (((0,), (0,)), ((), ()))
        gs[slot, :, :cols] = lax.dot_general(left, n[slot], dims, preferred_element_type=F32).astype(BF16)
        gs[slot, :, cols:] = lax.dot_general(low_part, low_part, dims, preferred_element_type=F32).astype(BF16)
        blocks(slot).start()

    each(STEPS * mats, gram_part)
    fetch_params().wait()

    def polys(slot):
        blocks(slot).wait_recv()
        top = gs[slot, :, :cols].astype(F32) + gr[slot, :, :cols].astype(F32)
        end = gs[slot, :, cols:].astype(F32) + gr[slot, :, cols:].astype(F32)
        eye = lax.broadcasted_iota(jnp.int32, (half, half), 0) == lax.broadcasted_iota(jnp.int32, (half, half), 1)
        trace = jnp.sum(jnp.where(eye, top[:, :half] + end, 0.0), keepdims=True)
        scale = 1.0 / (jnp.sqrt(trace) + 1e-07)
        square = scale * scale
        gram[:half, :] = top * square
        gram[half:, half:] = end * square
        gram[half:, :half] = (top[:, half:] * square).T
        low[...] = gram[...].astype(BF16)
        for it in range(NS_ITERS):
            def make_poly(t):
                r = pl.ds(pl.multiple_of(t * half, half), half)
                poly[it, r] = (COEF_B * low[r].astype(F32) + COEF_C * dot(low[r], low[...])).astype(BF16)

            def make_right(t):
                r = pl.ds(pl.multiple_of(t * half, half), half)
                value = COEF_A * gram[r] + dot(low[r], poly[it])
                right[r] = value
                rlow[r] = value.astype(BF16)

            def make_gram(t):
                r = pl.ds(pl.multiple_of(t * half, half), half)
                value = COEF_A * right[r] + dot(poly[it, r], rlow[...])
                gram[r] = value
                low[r] = value.astype(BF16)

            each(2, make_poly)
            if it < NS_ITERS - 1:
                each(2, make_right)
                each(2, make_gram)
        return scale

    def update(slot, r, scale):
        ycur = (n[slot, r].astype(F32) * scale).astype(BF16)
        for it in range(NS_ITERS):
            ycur = COEF_A * ycur.astype(F32) + dot(ycur, poly[it])
            if it < NS_ITERS - 1:
                ycur = ycur.astype(BF16)
        return ycur

    def step_one(i):
        scale = polys(i)

        def body(c):
            r = part(c)
            l1[i, r] = (p[i, r].astype(F32) - step_scale * update(i, r, scale)).astype(BF16)
            third(i, r).start()

        each(per, body)

    each(mats, step_one)

    third(0, pl.ds(0, rows)).wait_recv()

    def pair_mean(r):
        p1[r] = mean(l1[0, r], rl1[0, r])

    pieces(0, rows, pair_mean)
    share_p().start()

    def step_two(i):
        scale = polys(mats + i)
        third(i, pl.ds(0, rows)).wait_recv()

        def body(c):
            r = part(c)
            cur = mean(l1[i, r], rl1[i, r]).astype(F32)
            l2[i, r] = (cur - step_scale * update(mats + i, r, scale)).astype(BF16)
            fourth(i, r, i * (1 - c // (per - 1)) if i == mats - 1 else i).start()

        each(per, body)

    for i in range(1, mats):
        step_two(i)

    share_m().wait_recv()
    pass_m().start()
    raw(g.at[1, 0], pl.ds(0, rows)).wait_recv()
    pass_m().wait_recv()

    def momentum_far(r):
        grad = gb[r].astype(F32)
        new = (BETA * m1b[r].astype(F32) + grad).astype(BF16)
        n[spare, r] = (grad + BETA * new.astype(F32)).astype(BF16)
        m_out[0, 0, r] = mean(mn2[0, r], new)

    pieces(0, rows, momentum_far)
    gram_part(spare)

    own_scale = polys(mats)

    def own(c):
        r = part(c)
        l2[0, r] = (p1[r].astype(F32) - step_scale * update(mats, r, own_scale)).astype(BF16)

    each(per, own)

    far_scale = polys(spare)
    share_p().wait_recv()
    pass_p().start()
    pass_p().wait_recv()

    def theirs(c):
        r = part(c)
        local = (p1b[r].astype(F32) - step_scale * update(spare, r, far_scale)).astype(BF16)
        p_out[0, 0, r] = mean(l2[0, r], local)

    each(per, theirs)

    second(others, pl.ds(0, rows)).wait_recv()
    for i in range(1, mats):
        def momentum_out(r):
            m_out[0, i, r] = mean(mn2[i, r], rm2[i, r])

        pieces(0, rows, momentum_out)

    for seg in range(segs):
        first(*place(seg), seg).wait_send()
    for copy in (raw(g.at[1, 0], pl.ds(0, rows)), second(others, pl.ds(0, rows)), share_m(), pass_m(), share_p(), pass_p()):
        copy.wait_send()
    for i in range(mats):
        third(i, pl.ds(0, rows)).wait_send()
    each(STEPS * mats + 1, lambda slot: blocks(slot).wait_send())

    for i in range(1, mats):
        ends = [(0, rows - chunk, i), (rows - chunk, chunk, 0)] if i == mats - 1 else [(0, rows, i)]
        for start, size, at in ends:
            fourth(i, pl.ds(start, size), at).wait_recv()

            def params_out(r):
                p_out[0, i, r] = mean(l2[i, r], rl2[i, r])

            pieces(start, size, params_out)
    fourth(others, pl.ds(0, rows), 0).wait_send()


def put(p, m, p_out, m_out, sem):
    copies = [
        pltpu.make_async_copy(src.at[0, i], dst.at[0, i], sem.at[k, i])
        for k, (src, dst) in enumerate(((p, p_out), (m, m_out))) for i in range(p.shape[1])
    ]
    for copy in copies:
        copy.start()
    for copy in copies:
        copy.wait()


def fused(params, momentum, grads):
    _, mats, rows, cols = params.shape
    seg_rows, chunk = min(SEG, rows // 2), min(CHUNK, rows // 2)
    whole, one = pltpu.VMEM((mats, rows, cols), BF16), pltpu.VMEM((rows, cols), BF16)
    slots = STEPS * mats + 1
    pack = pltpu.VMEM((slots, cols // 2, cols + cols // 2), BF16)
    small, small_low = pltpu.VMEM((cols, cols), F32), pltpu.VMEM((cols, cols), BF16)
    dma = pltpu.SemaphoreType.DMA
    segs = mats * (rows // seg_rows)
    anywhere = pl.BlockSpec(memory_space=pl.ANY)
    results = pl.pallas_call(
        functools.partial(kernel, seg_rows, chunk),
        out_shape=[pltpu.VMEM(params.shape, BF16)] * 2,
        in_specs=[anywhere] * 3,
        out_specs=[pl.BlockSpec(memory_space=pltpu.VMEM)] * 2,
        scratch_shapes=[
            whole, whole, pltpu.VMEM((STEPS, mats, rows, cols), BF16),
            whole, whole, whole, whole, pltpu.VMEM((slots, rows, cols), BF16),
            whole, whole, whole, whole, one, one, one, one, one, pack, pack,
            small, small_low, pltpu.VMEM((NS_ITERS, cols, cols), BF16), small, small_low,
            dma((3, segs)), dma(()), dma((segs,)), dma((2,)), dma((mats,)), dma((mats,)), dma((slots,)), dma((4,)),
            dma((10,)), pltpu.SemaphoreType.REGULAR((2,)),
        ],
        compiler_params=pltpu.CompilerParams(
            collective_id=0, has_side_effects=True, vmem_limit_bytes=59 * 2**20),
    )(params, momentum, grads)
    return pl.pallas_call(
        put,
        out_shape=[jax.ShapeDtypeStruct(params.shape, BF16)] * 2,
        in_specs=[pl.BlockSpec(memory_space=pltpu.VMEM)] * 2,
        out_specs=[anywhere] * 2,
        scratch_shapes=[dma((2, mats))],
        compiler_params=pltpu.CompilerParams(vmem_limit_bytes=2**20),
    )(*[pltpu.with_memory_space_constraint(r, pltpu.VMEM) for r in results])


def solution(mesh):
    def program(params, momentum, grads):
        paired = mesh.shape["fsdp"] == 2 and params.shape[1] > 1
        return (fused if paired else shards)(params, momentum, grads)

    return jax.shard_map(
        program,
        mesh=mesh,
        in_specs=(
            P("replica", None, "fsdp", None),
            P("replica", None, "fsdp", None),
            P(None, "replica", None, "fsdp", None),
        ),
        out_specs=(P("replica", None, "fsdp", None), P("replica", None, "fsdp", None)),
        check_vma=False,
    )
```

```python
import functools
import math

import jax
import jax.numpy as jnp
from jax import lax
from jax.experimental import pallas as pl
from jax.experimental.pallas import tpu as pltpu
from jax.sharding import PartitionSpec as P

ROWS = 2048
COLS = 512
NS_ITERS = 3
STEPS = 2


BETA = 0.95
LEARN = 0.5
COEF_A = 3.4445
COEF_B = -4.775
COEF_C = 2.0315

MESH = pl.DeviceIdType.MESH
BF16 = jnp.bfloat16
F32 = jnp.float32


def partner(value, axis, apart):
    mask = 2**apart
    pairs = [(source, source ^ mask) for source in range(lax.axis_size(axis))]
    return lax.ppermute(value, axis, pairs)


def dot(a, b):
    return jnp.dot(a, b, preferred_element_type=F32)


def reduce_gram(nest):
    part = lax.dot_general(nest, nest, (((0,), (0,)), ((), ())), preferred_element_type=F32)
    half = part.shape[0] // 2
    packed = jnp.concatenate([part[:half], part[half:, half:]], axis=1).astype(BF16)
    if lax.axis_size("fsdp") == 2:
        whole = packed.astype(F32) + partner(packed, "fsdp", 0).astype(F32)
    else:
        whole = lax.psum(packed.astype(F32), "fsdp")
    top, low = whole[:, : 2 * half], whole[:, 2 * half :]
    return jnp.concatenate([top, jnp.concatenate([top[:, half:].T, low], axis=1)], axis=0)


def orthogonalize(nest, gram):
    scale = 1.0 / (jnp.sqrt(jnp.trace(gram)) + 1e-07)
    gram = gram * (scale * scale)
    ycur = (nest.astype(F32) * scale).astype(BF16)
    for it in range(NS_ITERS):
        low = gram.astype(BF16)
        poly = (COEF_B * low.astype(F32) + COEF_C * dot(low, low)).astype(BF16)
        if it < NS_ITERS - 1:
            right = COEF_A * gram + dot(low, poly)
            gram = COEF_A * right + dot(poly, right.astype(BF16))
        ycur = COEF_A * ycur.astype(F32) + dot(ycur, poly)
        if it < NS_ITERS - 1:
            ycur = ycur.astype(BF16)
    return ycur


def mean(a, b):
    return (0.5 * (a.astype(F32) + b.astype(F32))).astype(BF16)


def shards(params, momentum, grads):
    mats = params.shape[1]
    step_scale = LEARN * 0.2 * math.sqrt(max(ROWS, COLS))
    nests = []
    mcur = [momentum[0, i] for i in range(mats)]
    for step in range(STEPS):
        grad = [grads[step, 0, i].astype(F32) for i in range(mats)]
        m_new = [(BETA * m.astype(F32) + g).astype(BF16) for m, g in zip(mcur, grad)]
        nests.append([(g + BETA * m.astype(F32)).astype(BF16) for m, g in zip(m_new, grad)])
        mcur = [mean(m, partner(m, "replica", step)) for m in m_new]
    grams = [[reduce_gram(n) for n in row] for row in nests]
    pcur = [params[0, i] for i in range(mats)]
    for step in range(STEPS):
        for i in range(mats):
            update = orthogonalize(nests[step][i], grams[step][i])
            local = (pcur[i].astype(F32) - step_scale * update).astype(BF16)
            pcur[i] = mean(local, partner(local, "replica", step))
    return (jnp.stack(pcur)[None], jnp.stack(mcur)[None])


SUB = 64
HEAD = 128
CHUNK = 256


def kernel(chunk, p_hbm, m_hbm, g_hbm, p_out, m_out,
           p, m, g, mn1, rm1, mn2, rm2, n, l1, rl1, l2, rl2,
           m1, m1b, p1, p1b, gb, gs, gr, gram, low, poly, right, rlow,
           isem, msem, esem, lsem, usem, bsem, wsem, osem, hsem):
    mats, rows, cols = p.shape
    half = cols // 2
    share = rows // 2
    per = rows // chunk
    spare = STEPS * mats
    step_scale = LEARN * 0.2 * math.sqrt(max(ROWS, COLS))
    side = lax.axis_index("fsdp")
    rep = lax.axis_index("replica")
    core = rep % 2
    late = (rep // 2) % 2
    across = {"fsdp": 1 - side}
    near = {"replica": rep + 1 - 2 * core}
    far = {"replica": rep + 2 - 4 * late}
    mine = pl.ds(pl.multiple_of(core * share, share), share)
    others = pl.ds(1, mats - 1)

    def each(total, body):
        lax.fori_loop(0, total, lambda k, c: (body(k), c)[1], 0)

    def part(c):
        return pl.ds(pl.multiple_of(c * chunk, chunk), chunk)

    everything = pl.ds(0, rows)

    def pieces(start, size, body):
        each(size // SUB, lambda k: body(pl.ds(pl.multiple_of(start + k * SUB, SUB), SUB)))

    def mean(a, b):
        return (0.5 * (a.astype(F32) + b.astype(F32))).astype(BF16)

    heads = [pl.ds(0, HEAD), pl.ds(HEAD, rows - HEAD)]

    def fetch_raw(k):
        return pltpu.make_async_copy(g_hbm.at[1, 0, 0, heads[k]], g.at[1, 0, heads[k]], isem.at[k])

    def fetch_momentum():
        return pltpu.make_async_copy(m_hbm.at[0], m, isem.at[2])

    def fetch_params():
        return pltpu.make_async_copy(p_hbm.at[0], p, isem.at[2])

    def fetch_first():
        return pltpu.make_async_copy(g_hbm.at[0, 0, 0], g.at[0, 0], isem.at[3])

    def fetch_others():
        return pltpu.make_async_copy(g_hbm.at[:, 0, others], g.at[:, others], isem.at[4])

    def send(src, dst, sent, got, peer):
        return pltpu.make_async_remote_copy(
            src_ref=src, dst_ref=dst, send_sem=sent, recv_sem=got, device_id=peer, device_id_type=MESH)

    def raw(src, r):
        return send(src, gb.at[r], osem.at[0], wsem.at[0], far)

    def first(i):
        return send(mn1.at[i], rm1.at[i], osem.at[1], msem.at[i], near)

    def second(i):
        return send(mn2.at[i], rm2.at[i], osem.at[0], wsem.at[1], far)

    def share_m():
        return send(m1.at[mine], m1b.at[mine], osem.at[0], wsem.at[2], far)

    def pass_m():
        return send(m1b.at[mine], m1b.at[mine], osem.at[1], esem.at[0], near)

    def third(i, r):
        return send(l1.at[i, r], rl1.at[i, r], osem.at[1], lsem.at[0], near)

    def share_p():
        return send(p1.at[mine], p1b.at[mine], osem.at[0], wsem.at[3], far)

    def pass_p():
        return send(p1b.at[mine], p1b.at[mine], osem.at[1], esem.at[1], near)

    def fourth(i, r, at):
        return send(l2.at[i, r], rl2.at[i, r], osem.at[0], usem.at[at], far)

    def blocks(slot):
        return send(gs.at[slot], gr.at[slot], osem.at[2], bsem.at[slot], across)

    barrier = pltpu.get_barrier_semaphore()
    pl.semaphore_signal(barrier, inc=1, device_id=far, device_id_type=MESH)

    @pl.when(late == 0)
    def _():
        for peer in (near, across):
            pl.semaphore_signal(barrier, inc=1, device_id=peer, device_id_type=MESH)

    def fetch_rest():
        fetch_momentum().start()
        fetch_first().start()
        fetch_others().start()

    @pl.when(late == 0)
    def _():
        for k in range(2):
            fetch_raw(k).start()
        fetch_rest()
        for k in range(2):
            fetch_raw(k).wait()
        pl.semaphore_wait(barrier, 3)
        for r in heads:
            raw(g.at[1, 0, r], r).start()
        for peer in (near, across):
            pl.semaphore_signal(hsem.at[0], inc=1, device_id=peer, device_id_type=MESH)

    @pl.when(late == 1)
    def _():
        pl.semaphore_wait(barrier, 1)
        raw(g_hbm.at[1, 0, 0, heads[0]], heads[0]).start()
        for k in (1, 0):
            fetch_raw(k).start()
        fetch_raw(1).wait()
        raw(g.at[1, 0, heads[1]], heads[1]).start()
        fetch_rest()
        fetch_raw(0).wait()

    def meet():
        @pl.when(late == 0)
        def _():
            pl.semaphore_wait(hsem.at[0], 2)
            pl.semaphore_signal(hsem.at[1], inc=1, device_id=far, device_id_type=MESH)

        @pl.when(late == 1)
        def _():
            pl.semaphore_wait(hsem.at[1], 1)

    def momentum_one(i):
        if i == 0:
            fetch_momentum().wait()
            fetch_first().wait()
        if i == 1:
            fetch_others().wait()

        def body(r):
            grad = g[0, i, r].astype(F32)
            new = (BETA * m[i, r].astype(F32) + grad).astype(BF16)
            mn1[i, r] = new
            n[i, r] = (grad + BETA * new.astype(F32)).astype(BF16)

        pieces(0, rows, body)
        if i == 0:
            meet()
            fetch_params().start()
        first(i).start()

    def momentum_two(i):
        first(i).wait_recv()

        def body(r):
            grad = g[1, i, r].astype(F32)
            cur = mean(mn1[i, r], rm1[i, r])
            if i == 0:
                m1[r] = cur
            new = (BETA * cur.astype(F32) + grad).astype(BF16)
            mn2[i, r] = new
            n[mats + i, r] = (grad + BETA * new.astype(F32)).astype(BF16)

        pieces(0, rows, body)
        (second(i) if i > 0 else share_m()).start()

    for i in range(mats + 1):
        if i < mats:
            momentum_one(i)
        if i > 0:
            momentum_two(i - 1)

    def gram_part(slot):
        left, low_part = n[slot, :, :half], n[slot, :, half:]
        dims = (((0,), (0,)), ((), ()))
        gs[slot, :, :cols] = lax.dot_general(left, n[slot], dims, preferred_element_type=F32).astype(BF16)
        gs[slot, :, cols:] = lax.dot_general(low_part, low_part, dims, preferred_element_type=F32).astype(BF16)
        blocks(slot).start()

    each(STEPS * mats, gram_part)
    fetch_params().wait()

    def polys(slot):
        blocks(slot).wait_recv()
        top = gs[slot, :, :cols].astype(F32) + gr[slot, :, :cols].astype(F32)
        end = gs[slot, :, cols:].astype(F32) + gr[slot, :, cols:].astype(F32)
        eye = lax.broadcasted_iota(jnp.int32, (half, half), 0) == lax.broadcasted_iota(jnp.int32, (half, half), 1)
        trace = jnp.sum(jnp.where(eye, top[:, :half] + end, 0.0), keepdims=True)
        scale = 1.0 / (jnp.sqrt(trace) + 1e-07)
        square = scale * scale
        gram[:half, :] = top * square
        gram[half:, half:] = end * square
        gram[half:, :half] = (top[:, half:] * square).T
        low[...] = gram[...].astype(BF16)
        for it in range(NS_ITERS):
            def make_poly(t):
                r = pl.ds(pl.multiple_of(t * half, half), half)
                poly[it, r] = (COEF_B * low[r].astype(F32) + COEF_C * dot(low[r], low[...])).astype(BF16)

            def make_right(t):
                r = pl.ds(pl.multiple_of(t * half, half), half)
                value = COEF_A * gram[r] + dot(low[r], poly[it])
                right[r] = value
                rlow[r] = value.astype(BF16)

            def make_gram(t):
                r = pl.ds(pl.multiple_of(t * half, half), half)
                value = COEF_A * right[r] + dot(poly[it, r], rlow[...])
                gram[r] = value
                low[r] = value.astype(BF16)

            each(2, make_poly)
            if it < NS_ITERS - 1:
                each(2, make_right)
                each(2, make_gram)
        return scale

    def update(slot, r, scale):
        ycur = (n[slot, r].astype(F32) * scale).astype(BF16)
        for it in range(NS_ITERS):
            ycur = COEF_A * ycur.astype(F32) + dot(ycur, poly[it])
            if it < NS_ITERS - 1:
                ycur = ycur.astype(BF16)
        return ycur

    def step_one(i):
        scale = polys(i)

        def body(c):
            r = part(c)
            l1[i, r] = (p[i, r].astype(F32) - step_scale * update(i, r, scale)).astype(BF16)
            third(i, r).start()

        each(per, body)

    each(mats, step_one)

    third(pl.ds(0, mats), everything).wait_recv()

    def pair_mean(r):
        p1[r] = mean(l1[0, r], rl1[0, r])

    pieces(0, rows, pair_mean)
    share_p().start()

    def step_two(i):
        scale = polys(mats + i)

        def body(c):
            r = part(c)
            cur = mean(l1[i, r], rl1[i, r]).astype(F32)
            l2[i, r] = (cur - step_scale * update(mats + i, r, scale)).astype(BF16)
            fourth(i, r, i * (1 - c // (per - 1)) if i == mats - 1 else i).start()

        each(per, body)

    for i in range(1, mats):
        step_two(i)

    share_m().wait_recv()
    pass_m().start()
    raw(g.at[1, 0], everything).wait_recv()
    pass_m().wait_recv()

    def momentum_far(r):
        grad = gb[r].astype(F32)
        new = (BETA * m1b[r].astype(F32) + grad).astype(BF16)
        n[spare, r] = (grad + BETA * new.astype(F32)).astype(BF16)
        m_out[0, 0, r] = mean(mn2[0, r], new)

    pieces(0, rows, momentum_far)
    gram_part(spare)

    own_scale = polys(mats)

    def own(c):
        r = part(c)
        l2[0, r] = (p1[r].astype(F32) - step_scale * update(mats, r, own_scale)).astype(BF16)

    each(per, own)

    far_scale = polys(spare)
    share_p().wait_recv()
    pass_p().start()
    pass_p().wait_recv()

    def theirs(c):
        r = part(c)
        local = (p1b[r].astype(F32) - step_scale * update(spare, r, far_scale)).astype(BF16)
        p_out[0, 0, r] = mean(l2[0, r], local)

    each(per, theirs)

    second(others).wait_recv()
    for i in range(1, mats):
        def momentum_out(r):
            m_out[0, i, r] = mean(mn2[i, r], rm2[i, r])

        pieces(0, rows, momentum_out)

    def sent(ref, sem, peer):
        return send(ref, ref, sem, usem.at[0], peer)

    sent(n, osem.at[1], near).wait_send()
    sent(gs, osem.at[2], across).wait_send()

    for i in range(1, mats):
        ends = [(0, rows - chunk, i), (rows - chunk, chunk, 0)] if i == mats - 1 else [(0, rows, i)]
        for start, size, at in ends:
            fourth(i, pl.ds(start, size), at).wait_recv()

            def params_out(r):
                p_out[0, i, r] = mean(l2[i, r], rl2[i, r])

            pieces(start, size, params_out)
    sent(n.at[pl.ds(0, STEPS * mats)], osem.at[0], far).wait_send()


def put(p, m, p_out, m_out, sem):
    copies = [pltpu.make_async_copy(src, dst, sem.at[k]) for k, (src, dst) in enumerate(((p, p_out), (m, m_out)))]
    for copy in copies:
        copy.start()
    for copy in copies:
        copy.wait()


def fused(params, momentum, grads):
    _, mats, rows, cols = params.shape
    chunk = min(CHUNK, rows // 2)
    whole, one = pltpu.VMEM((mats, rows, cols), BF16), pltpu.VMEM((rows, cols), BF16)
    slots = STEPS * mats + 1
    pack = pltpu.VMEM((slots, cols // 2, cols + cols // 2), BF16)
    small, small_low = pltpu.VMEM((cols, cols), F32), pltpu.VMEM((cols, cols), BF16)
    dma = pltpu.SemaphoreType.DMA
    anywhere = pl.BlockSpec(memory_space=pl.ANY)
    results = pl.pallas_call(
        functools.partial(kernel, chunk),
        out_shape=[pltpu.VMEM(params.shape, BF16)] * 2,
        in_specs=[anywhere] * 3,
        out_specs=[pl.BlockSpec(memory_space=pltpu.VMEM)] * 2,
        scratch_shapes=[
            whole, whole, pltpu.VMEM((STEPS, mats, rows, cols), BF16),
            whole, whole, whole, whole, pltpu.VMEM((slots, rows, cols), BF16),
            whole, whole, whole, whole, one, one, one, one, one, pack, pack,
            small, small_low, pltpu.VMEM((NS_ITERS, cols, cols), BF16), small, small_low,
            dma((5,)), dma((mats,)), dma((2,)), dma((1,)), dma((mats,)), dma((slots,)), dma((4,)), dma((3,)),
            pltpu.SemaphoreType.REGULAR((2,)),
        ],
        compiler_params=pltpu.CompilerParams(
            collective_id=0, has_side_effects=True, vmem_limit_bytes=59 * 2**20),
    )(params, momentum, grads)
    return pl.pallas_call(
        put,
        out_shape=[jax.ShapeDtypeStruct(params.shape, BF16)] * 2,
        in_specs=[pl.BlockSpec(memory_space=pltpu.VMEM)] * 2,
        out_specs=[anywhere] * 2,
        scratch_shapes=[dma((2,))],
        compiler_params=pltpu.CompilerParams(vmem_limit_bytes=2**20),
    )(*[pltpu.with_memory_space_constraint(r, pltpu.VMEM) for r in results])


def solution(mesh):
    def program(params, momentum, grads):
        paired = mesh.shape["fsdp"] == 2 and params.shape[1] > 1
        return (fused if paired else shards)(params, momentum, grads)

    return jax.shard_map(
        program,
        mesh=mesh,
        in_specs=(
            P("replica", None, "fsdp", None),
            P("replica", None, "fsdp", None),
            P(None, "replica", None, "fsdp", None),
        ),
        out_specs=(P("replica", None, "fsdp", None), P("replica", None, "fsdp", None)),
        check_vma=False,
    )
```

```python
import functools
import math

import jax
import jax.numpy as jnp
from jax import lax
from jax.experimental import pallas as pl
from jax.experimental.pallas import tpu as pltpu
from jax.sharding import PartitionSpec as P

ROWS = 2048
COLS = 512
NS_ITERS = 3
STEPS = 2


BETA = 0.95
LEARN = 0.5
COEF_A = 3.4445
COEF_B = -4.775
COEF_C = 2.0315

MESH = pl.DeviceIdType.MESH
BF16 = jnp.bfloat16
F32 = jnp.float32


def partner(value, axis, apart):
    mask = 2**apart
    pairs = [(source, source ^ mask) for source in range(lax.axis_size(axis))]
    return lax.ppermute(value, axis, pairs)


def dot(a, b):
    return jnp.dot(a, b, preferred_element_type=F32)


def reduce_gram(nest):
    part = lax.dot_general(nest, nest, (((0,), (0,)), ((), ())), preferred_element_type=F32)
    half = part.shape[0] // 2
    packed = jnp.concatenate([part[:half], part[half:, half:]], axis=1).astype(BF16)
    if lax.axis_size("fsdp") == 2:
        whole = packed.astype(F32) + partner(packed, "fsdp", 0).astype(F32)
    else:
        whole = lax.psum(packed.astype(F32), "fsdp")
    top, low = whole[:, : 2 * half], whole[:, 2 * half :]
    return jnp.concatenate([top, jnp.concatenate([top[:, half:].T, low], axis=1)], axis=0)


def orthogonalize(nest, gram):
    scale = 1.0 / (jnp.sqrt(jnp.trace(gram)) + 1e-07)
    gram = gram * (scale * scale)
    ycur = (nest.astype(F32) * scale).astype(BF16)
    for it in range(NS_ITERS):
        low = gram.astype(BF16)
        poly = (COEF_B * low.astype(F32) + COEF_C * dot(low, low)).astype(BF16)
        if it < NS_ITERS - 1:
            right = COEF_A * gram + dot(low, poly)
            gram = COEF_A * right + dot(poly, right.astype(BF16))
        ycur = COEF_A * ycur.astype(F32) + dot(ycur, poly)
        if it < NS_ITERS - 1:
            ycur = ycur.astype(BF16)
    return ycur


def mean(a, b):
    return (0.5 * (a.astype(F32) + b.astype(F32))).astype(BF16)


def shards(params, momentum, grads):
    mats = params.shape[1]
    step_scale = LEARN * 0.2 * math.sqrt(max(ROWS, COLS))
    nests = []
    mcur = [momentum[0, i] for i in range(mats)]
    for step in range(STEPS):
        grad = [grads[step, 0, i].astype(F32) for i in range(mats)]
        m_new = [(BETA * m.astype(F32) + g).astype(BF16) for m, g in zip(mcur, grad)]
        nests.append([(g + BETA * m.astype(F32)).astype(BF16) for m, g in zip(m_new, grad)])
        mcur = [mean(m, partner(m, "replica", step)) for m in m_new]
    grams = [[reduce_gram(n) for n in row] for row in nests]
    pcur = [params[0, i] for i in range(mats)]
    for step in range(STEPS):
        for i in range(mats):
            update = orthogonalize(nests[step][i], grams[step][i])
            local = (pcur[i].astype(F32) - step_scale * update).astype(BF16)
            pcur[i] = mean(local, partner(local, "replica", step))
    return (jnp.stack(pcur)[None], jnp.stack(mcur)[None])


SUB = 64
HEAD = 128
SKEW = 48
CHUNK = 256


def kernel(chunk, p_hbm, m_hbm, g_hbm, p_out, m_out,
           p, m, g, mn1, rm1, mn2, rm2, n, l1, rl1, l2, rl2,
           m1, m1b, p1, p1b, gb, gs, gr, gram, low, poly, right, rlow,
           isem, msem, esem, lsem, usem, bsem, wsem, osem, hsem):
    mats, rows, cols = p.shape
    half = cols // 2
    per = rows // chunk
    spare = STEPS * mats
    step_scale = LEARN * 0.2 * math.sqrt(max(ROWS, COLS))
    side = lax.axis_index("fsdp")
    rep = lax.axis_index("replica")
    core = rep % 2
    late = (rep // 2) % 2
    across = {"fsdp": 1 - side}
    near = {"replica": rep + 1 - 2 * core}
    far = {"replica": rep + 2 - 4 * late}
    cut = rows // 2 - SKEW
    parts = [pl.ds(0, cut), pl.ds(cut, rows - cut)]
    others = pl.ds(1, mats - 1)

    def each(total, body):
        lax.fori_loop(0, total, lambda k, c: (body(k), c)[1], 0)

    def part(c):
        return pl.ds(pl.multiple_of(c * chunk, chunk), chunk)

    everything = pl.ds(0, rows)

    def pieces(start, size, body):
        each(size // SUB, lambda k: body(pl.ds(pl.multiple_of(start + k * SUB, SUB), SUB)))

    def mean(a, b):
        return (0.5 * (a.astype(F32) + b.astype(F32))).astype(BF16)

    heads = [pl.ds(0, HEAD), pl.ds(HEAD, rows - HEAD)]

    def fetch_raw(k):
        return pltpu.make_async_copy(g_hbm.at[1, 0, 0, heads[k]], g.at[1, 0, heads[k]], isem.at[k])

    def fetch_momentum():
        return pltpu.make_async_copy(m_hbm.at[0], m, isem.at[2])

    def fetch_params():
        return pltpu.make_async_copy(p_hbm.at[0], p, isem.at[2])

    def fetch_first():
        return pltpu.make_async_copy(g_hbm.at[0, 0, 0], g.at[0, 0], isem.at[3])

    def fetch_others():
        return pltpu.make_async_copy(g_hbm.at[:, 0, others], g.at[:, others], isem.at[4])

    def send(src, dst, sent, got, peer):
        return pltpu.make_async_remote_copy(
            src_ref=src, dst_ref=dst, send_sem=sent, recv_sem=got, device_id=peer, device_id_type=MESH)

    def raw(src, r):
        return send(src, gb.at[r], osem.at[0], wsem.at[0], far)

    def first(i):
        return send(mn1.at[i], rm1.at[i], osem.at[1], msem.at[i], near)

    def second(i):
        return send(mn2.at[i], rm2.at[i], osem.at[0], wsem.at[1], far)

    def by_core(body):
        for c in range(2):
            @pl.when(core == c)
            def _(c=c):
                body(parts[c], parts[1 - c])

    def share_m(r):
        return send(m1.at[r], m1b.at[r], osem.at[0], wsem.at[2], far)

    def pass_m(r):
        return send(m1b.at[r], m1b.at[r], osem.at[1], esem.at[0], near)

    def third(i, r):
        return send(l1.at[i, r], rl1.at[i, r], osem.at[1], lsem.at[0], near)

    def share_p(r):
        return send(p1.at[r], p1b.at[r], osem.at[0], wsem.at[3], far)

    def pass_p(r):
        return send(p1b.at[r], p1b.at[r], osem.at[1], esem.at[1], near)

    def fourth(i, r, at):
        return send(l2.at[i, r], rl2.at[i, r], osem.at[0], usem.at[at], far)

    def blocks(slot):
        return send(gs.at[slot], gr.at[slot], osem.at[2], bsem.at[slot], across)

    barrier = pltpu.get_barrier_semaphore()
    pl.semaphore_signal(barrier, inc=1, device_id=far, device_id_type=MESH)

    @pl.when(late == 0)
    def _():
        for peer in (near, across):
            pl.semaphore_signal(barrier, inc=1, device_id=peer, device_id_type=MESH)

    def fetch_rest():
        fetch_momentum().start()
        fetch_first().start()
        fetch_others().start()

    @pl.when(late == 0)
    def _():
        for k in range(2):
            fetch_raw(k).start()
        fetch_rest()
        for k in range(2):
            fetch_raw(k).wait()
        pl.semaphore_wait(barrier, 3)
        for r in heads:
            raw(g.at[1, 0, r], r).start()
        for peer in (near, across):
            pl.semaphore_signal(hsem.at[0], inc=1, device_id=peer, device_id_type=MESH)

    @pl.when(late == 1)
    def _():
        pl.semaphore_wait(barrier, 1)
        raw(g_hbm.at[1, 0, 0, heads[0]], heads[0]).start()
        for k in (1, 0):
            fetch_raw(k).start()
        fetch_raw(1).wait()
        raw(g.at[1, 0, heads[1]], heads[1]).start()
        fetch_rest()
        fetch_raw(0).wait()

    def meet():
        @pl.when(late == 0)
        def _():
            pl.semaphore_wait(hsem.at[0], 2)
            pl.semaphore_signal(hsem.at[1], inc=1, device_id=far, device_id_type=MESH)

        @pl.when(late == 1)
        def _():
            pl.semaphore_wait(hsem.at[1], 1)

    def momentum_one(i):
        if i == 0:
            fetch_momentum().wait()
            fetch_first().wait()
        if i == 1:
            fetch_others().wait()

        def body(r):
            grad = g[0, i, r].astype(F32)
            new = (BETA * m[i, r].astype(F32) + grad).astype(BF16)
            mn1[i, r] = new
            n[i, r] = (grad + BETA * new.astype(F32)).astype(BF16)

        pieces(0, rows, body)
        if i == 0:
            meet()
            fetch_params().start()
        first(i).start()

    def momentum_two(i):
        first(i).wait_recv()

        def body(r):
            grad = g[1, i, r].astype(F32)
            cur = mean(mn1[i, r], rm1[i, r])
            if i == 0:
                m1[r] = cur
            new = (BETA * cur.astype(F32) + grad).astype(BF16)
            mn2[i, r] = new
            n[mats + i, r] = (grad + BETA * new.astype(F32)).astype(BF16)

        pieces(0, rows, body)
        if i > 0:
            second(i).start()
        else:
            by_core(lambda own, other: share_m(own).start())

    for i in range(mats + 1):
        if i < mats:
            momentum_one(i)
        if i > 0:
            momentum_two(i - 1)

    def gram_part(slot):
        left, low_part = n[slot, :, :half], n[slot, :, half:]
        dims = (((0,), (0,)), ((), ()))
        gs[slot, :, :cols] = lax.dot_general(left, n[slot], dims, preferred_element_type=F32).astype(BF16)
        gs[slot, :, cols:] = lax.dot_general(low_part, low_part, dims, preferred_element_type=F32).astype(BF16)
        blocks(slot).start()

    each(STEPS * mats, gram_part)
    fetch_params().wait()

    def polys(slot):
        blocks(slot).wait_recv()
        top = gs[slot, :, :cols].astype(F32) + gr[slot, :, :cols].astype(F32)
        end = gs[slot, :, cols:].astype(F32) + gr[slot, :, cols:].astype(F32)
        eye = lax.broadcasted_iota(jnp.int32, (half, half), 0) == lax.broadcasted_iota(jnp.int32, (half, half), 1)
        trace = jnp.sum(jnp.where(eye, top[:, :half] + end, 0.0), keepdims=True)
        scale = 1.0 / (jnp.sqrt(trace) + 1e-07)
        square = scale * scale
        gram[:half, :] = top * square
        gram[half:, half:] = end * square
        gram[half:, :half] = (top[:, half:] * square).T
        low[...] = gram[...].astype(BF16)
        for it in range(NS_ITERS):
            def make_poly(t):
                r = pl.ds(pl.multiple_of(t * half, half), half)
                poly[it, r] = (COEF_B * low[r].astype(F32) + COEF_C * dot(low[r], low[...])).astype(BF16)

            def make_right(t):
                r = pl.ds(pl.multiple_of(t * half, half), half)
                value = COEF_A * gram[r] + dot(low[r], poly[it])
                right[r] = value
                rlow[r] = value.astype(BF16)

            def make_gram(t):
                r = pl.ds(pl.multiple_of(t * half, half), half)
                value = COEF_A * right[r] + dot(poly[it, r], rlow[...])
                gram[r] = value
                low[r] = value.astype(BF16)

            each(2, make_poly)
            if it < NS_ITERS - 1:
                each(2, make_right)
                each(2, make_gram)
        return scale

    def update(slot, r, scale):
        ycur = (n[slot, r].astype(F32) * scale).astype(BF16)
        for it in range(NS_ITERS):
            ycur = COEF_A * ycur.astype(F32) + dot(ycur, poly[it])
            if it < NS_ITERS - 1:
                ycur = ycur.astype(BF16)
        return ycur

    def step_one(i):
        scale = polys(i)

        def body(c):
            r = part(c)
            l1[i, r] = (p[i, r].astype(F32) - step_scale * update(i, r, scale)).astype(BF16)
            third(i, r).start()

        each(per, body)

    each(mats, step_one)

    third(pl.ds(0, mats), everything).wait_recv()

    def pair_mean(r):
        p1[r] = mean(l1[0, r], rl1[0, r])

    pieces(0, rows, pair_mean)
    by_core(lambda own, other: share_p(own).start())

    def step_two(i):
        scale = polys(mats + i)

        def body(c):
            r = part(c)
            cur = mean(l1[i, r], rl1[i, r]).astype(F32)
            l2[i, r] = (cur - step_scale * update(mats + i, r, scale)).astype(BF16)
            fourth(i, r, i * (1 - c // (per - 1)) if i == mats - 1 else i).start()

        each(per, body)

    for i in range(1, mats):
        step_two(i)

    def join(share, hand):
        def body(own, other):
            share(own).wait_recv()
            hand(own).start()
            hand(other).wait_recv()

        by_core(body)

    raw(g.at[1, 0], everything).wait_recv()
    join(share_m, pass_m)

    def momentum_far(r):
        grad = gb[r].astype(F32)
        new = (BETA * m1b[r].astype(F32) + grad).astype(BF16)
        n[spare, r] = (grad + BETA * new.astype(F32)).astype(BF16)
        m_out[0, 0, r] = mean(mn2[0, r], new)

    pieces(0, rows, momentum_far)
    gram_part(spare)

    own_scale = polys(mats)

    def own(c):
        r = part(c)
        l2[0, r] = (p1[r].astype(F32) - step_scale * update(mats, r, own_scale)).astype(BF16)

    each(per, own)

    far_scale = polys(spare)
    join(share_p, pass_p)

    def theirs(c):
        r = part(c)
        local = (p1b[r].astype(F32) - step_scale * update(spare, r, far_scale)).astype(BF16)
        p_out[0, 0, r] = mean(l2[0, r], local)

    each(per, theirs)

    second(others).wait_recv()
    for i in range(1, mats):
        def momentum_out(r):
            m_out[0, i, r] = mean(mn2[i, r], rm2[i, r])

        pieces(0, rows, momentum_out)

    def sent(ref, sem, peer):
        return send(ref, ref, sem, usem.at[0], peer)

    sent(n.at[pl.ds(0, STEPS * mats)], osem.at[1], near).wait_send()
    by_core(lambda own, other: [hand(own).wait_send() for hand in (pass_m, pass_p)])
    sent(gs, osem.at[2], across).wait_send()

    for i in range(1, mats):
        ends = [(0, rows - chunk, i), (rows - chunk, chunk, 0)] if i == mats - 1 else [(0, rows, i)]
        for start, size, at in ends:
            fourth(i, pl.ds(start, size), at).wait_recv()

            def params_out(r):
                p_out[0, i, r] = mean(l2[i, r], rl2[i, r])

            pieces(start, size, params_out)
    sent(n.at[pl.ds(0, STEPS * mats - 1)], osem.at[0], far).wait_send()
    by_core(lambda own, other: [share(own).wait_send() for share in (share_m, share_p)])


def put(p, m, p_out, m_out, sem):
    copies = [pltpu.make_async_copy(src, dst, sem.at[k]) for k, (src, dst) in enumerate(((p, p_out), (m, m_out)))]
    for copy in copies:
        copy.start()
    for copy in copies:
        copy.wait()


def fused(params, momentum, grads):
    _, mats, rows, cols = params.shape
    chunk = min(CHUNK, rows // 2)
    whole, one = pltpu.VMEM((mats, rows, cols), BF16), pltpu.VMEM((rows, cols), BF16)
    slots = STEPS * mats + 1
    pack = pltpu.VMEM((slots, cols // 2, cols + cols // 2), BF16)
    small, small_low = pltpu.VMEM((cols, cols), F32), pltpu.VMEM((cols, cols), BF16)
    dma = pltpu.SemaphoreType.DMA
    anywhere = pl.BlockSpec(memory_space=pl.ANY)
    results = pl.pallas_call(
        functools.partial(kernel, chunk),
        out_shape=[pltpu.VMEM(params.shape, BF16)] * 2,
        in_specs=[anywhere] * 3,
        out_specs=[pl.BlockSpec(memory_space=pltpu.VMEM)] * 2,
        scratch_shapes=[
            whole, whole, pltpu.VMEM((STEPS, mats, rows, cols), BF16),
            whole, whole, whole, whole, pltpu.VMEM((slots, rows, cols), BF16),
            whole, whole, whole, whole, one, one, one, one, one, pack, pack,
            small, small_low, pltpu.VMEM((NS_ITERS, cols, cols), BF16), small, small_low,
            dma((5,)), dma((mats,)), dma((2,)), dma((1,)), dma((mats,)), dma((slots,)), dma((4,)), dma((3,)),
            pltpu.SemaphoreType.REGULAR((2,)),
        ],
        compiler_params=pltpu.CompilerParams(
            collective_id=0, has_side_effects=True, vmem_limit_bytes=59 * 2**20),
    )(params, momentum, grads)
    return pl.pallas_call(
        put,
        out_shape=[jax.ShapeDtypeStruct(params.shape, BF16)] * 2,
        in_specs=[pl.BlockSpec(memory_space=pltpu.VMEM)] * 2,
        out_specs=[anywhere] * 2,
        scratch_shapes=[dma((2,))],
        compiler_params=pltpu.CompilerParams(vmem_limit_bytes=2**20),
    )(*[pltpu.with_memory_space_constraint(r, pltpu.VMEM) for r in results])


def solution(mesh):
    def program(params, momentum, grads):
        paired = mesh.shape["fsdp"] == 2 and params.shape[1] > 1
        return (fused if paired else shards)(params, momentum, grads)

    return jax.shard_map(
        program,
        mesh=mesh,
        in_specs=(
            P("replica", None, "fsdp", None),
            P("replica", None, "fsdp", None),
            P(None, "replica", None, "fsdp", None),
        ),
        out_specs=(P("replica", None, "fsdp", None), P("replica", None, "fsdp", None)),
        check_vma=False,
    )
```

```python
import functools
import math

import jax
import jax.numpy as jnp
from jax import lax
from jax.experimental import pallas as pl
from jax.experimental.pallas import tpu as pltpu
from jax.sharding import PartitionSpec as P

ROWS = 2048
COLS = 512
NS_ITERS = 3
STEPS = 2


BETA = 0.95
LEARN = 0.5
COEF_A = 3.4445
COEF_B = -4.775
COEF_C = 2.0315

MESH = pl.DeviceIdType.MESH
BF16 = jnp.bfloat16
F32 = jnp.float32


def partner(value, axis, apart):
    mask = 2**apart
    pairs = [(source, source ^ mask) for source in range(lax.axis_size(axis))]
    return lax.ppermute(value, axis, pairs)


def dot(a, b):
    return jnp.dot(a, b, preferred_element_type=F32)


def reduce_gram(nest):
    part = lax.dot_general(nest, nest, (((0,), (0,)), ((), ())), preferred_element_type=F32)
    half = part.shape[0] // 2
    packed = jnp.concatenate([part[:half], part[half:, half:]], axis=1).astype(BF16)
    if lax.axis_size("fsdp") == 2:
        whole = packed.astype(F32) + partner(packed, "fsdp", 0).astype(F32)
    else:
        whole = lax.psum(packed.astype(F32), "fsdp")
    top, low = whole[:, : 2 * half], whole[:, 2 * half :]
    return jnp.concatenate([top, jnp.concatenate([top[:, half:].T, low], axis=1)], axis=0)


def orthogonalize(nest, gram):
    scale = 1.0 / (jnp.sqrt(jnp.trace(gram)) + 1e-07)
    gram = gram * (scale * scale)
    ycur = (nest.astype(F32) * scale).astype(BF16)
    for it in range(NS_ITERS):
        low = gram.astype(BF16)
        poly = (COEF_B * low.astype(F32) + COEF_C * dot(low, low)).astype(BF16)
        if it < NS_ITERS - 1:
            right = COEF_A * gram + dot(low, poly)
            gram = COEF_A * right + dot(poly, right.astype(BF16))
        ycur = COEF_A * ycur.astype(F32) + dot(ycur, poly)
        if it < NS_ITERS - 1:
            ycur = ycur.astype(BF16)
    return ycur


def mean(a, b):
    return (0.5 * (a.astype(F32) + b.astype(F32))).astype(BF16)


def shards(params, momentum, grads):
    mats = params.shape[1]
    step_scale = LEARN * 0.2 * math.sqrt(max(ROWS, COLS))
    nests = []
    mcur = [momentum[0, i] for i in range(mats)]
    for step in range(STEPS):
        grad = [grads[step, 0, i].astype(F32) for i in range(mats)]
        m_new = [(BETA * m.astype(F32) + g).astype(BF16) for m, g in zip(mcur, grad)]
        nests.append([(g + BETA * m.astype(F32)).astype(BF16) for m, g in zip(m_new, grad)])
        mcur = [mean(m, partner(m, "replica", step)) for m in m_new]
    grams = [[reduce_gram(n) for n in row] for row in nests]
    pcur = [params[0, i] for i in range(mats)]
    for step in range(STEPS):
        for i in range(mats):
            update = orthogonalize(nests[step][i], grams[step][i])
            local = (pcur[i].astype(F32) - step_scale * update).astype(BF16)
            pcur[i] = mean(local, partner(local, "replica", step))
    return (jnp.stack(pcur)[None], jnp.stack(mcur)[None])


SUB = 64
HEAD = 128
SKEW = 48
CHUNK = 256


def kernel(chunk, p_hbm, m_hbm, g_hbm, p_out, m_out, l2, rl2,
           p, m, g, mn1, rm1, mn2, rm2, n, l1, rl1,
           m1, m1b, p1, p1b, gb, gs, gr, gram, low, poly, right, rlow,
           isem, msem, esem, lsem, usem, bsem, wsem, osem, hsem):
    mats, rows, cols = p.shape
    half = cols // 2
    per = rows // chunk
    spare = STEPS * mats
    step_scale = LEARN * 0.2 * math.sqrt(max(ROWS, COLS))
    side = lax.axis_index("fsdp")
    rep = lax.axis_index("replica")
    core = rep % 2
    late = (rep // 2) % 2
    across = {"fsdp": 1 - side}
    near = {"replica": rep + 1 - 2 * core}
    far = {"replica": rep + 2 - 4 * late}
    cut = rows // 2 - SKEW
    parts = [pl.ds(0, cut), pl.ds(cut, rows - cut)]
    others = pl.ds(1, mats - 1)

    def each(total, body):
        lax.fori_loop(0, total, lambda k, c: (body(k), c)[1], 0)

    def part(c):
        return pl.ds(pl.multiple_of(c * chunk, chunk), chunk)

    everything = pl.ds(0, rows)

    def pieces(start, size, body):
        each(size // SUB, lambda k: body(pl.ds(pl.multiple_of(start + k * SUB, SUB), SUB)))

    def mean(a, b):
        return (0.5 * (a.astype(F32) + b.astype(F32))).astype(BF16)

    heads = [pl.ds(0, HEAD), pl.ds(HEAD, rows - HEAD)]

    def fetch_raw(k):
        return pltpu.make_async_copy(g_hbm.at[1, 0, 0, heads[k]], g.at[1, 0, heads[k]], isem.at[k])

    def fetch_momentum():
        return pltpu.make_async_copy(m_hbm.at[0], m, isem.at[2])

    def fetch_params():
        return pltpu.make_async_copy(p_hbm.at[0], p, isem.at[2])

    def fetch_first():
        return pltpu.make_async_copy(g_hbm.at[0, 0, 0], g.at[0, 0], isem.at[3])

    def fetch_others():
        return pltpu.make_async_copy(g_hbm.at[:, 0, others], g.at[:, others], isem.at[4])

    def send(src, dst, sent, got, peer):
        return pltpu.make_async_remote_copy(
            src_ref=src, dst_ref=dst, send_sem=sent, recv_sem=got, device_id=peer, device_id_type=MESH)

    def raw(src, r):
        return send(src, gb.at[r], osem.at[0], wsem.at[0], far)

    def first(i):
        return send(mn1.at[i], rm1.at[i], osem.at[1], msem.at[i], near)

    def second(i):
        return send(mn2.at[i], rm2.at[i], osem.at[0], wsem.at[1], far)

    def by_core(body):
        for c in range(2):
            @pl.when(core == c)
            def _(c=c):
                body(parts[c], parts[1 - c])

    def share_m(r):
        return send(m1.at[r], m1b.at[r], osem.at[0], wsem.at[2], far)

    def pass_m(r):
        return send(m1b.at[r], m1b.at[r], osem.at[1], esem.at[0], near)

    def third(i, r):
        return send(l1.at[i, r], rl1.at[i, r], osem.at[1], lsem.at[0], near)

    def share_p(r):
        return send(p1.at[r], p1b.at[r], osem.at[0], wsem.at[3], far)

    def pass_p(r):
        return send(p1b.at[r], p1b.at[r], osem.at[1], esem.at[1], near)

    def fourth(i, r, at):
        return send(l2.at[i, r], rl2.at[i, r], osem.at[0], usem.at[at], far)

    def blocks(slot):
        return send(gs.at[slot], gr.at[slot], osem.at[2], bsem.at[slot], across)

    barrier = pltpu.get_barrier_semaphore()
    pl.semaphore_signal(barrier, inc=1, device_id=far, device_id_type=MESH)

    @pl.when(late == 0)
    def _():
        for peer in (near, across):
            pl.semaphore_signal(barrier, inc=1, device_id=peer, device_id_type=MESH)

    def fetch_rest():
        fetch_momentum().start()
        fetch_first().start()
        fetch_others().start()

    @pl.when(late == 0)
    def _():
        for k in range(2):
            fetch_raw(k).start()
        fetch_rest()
        for k in range(2):
            fetch_raw(k).wait()
        pl.semaphore_wait(barrier, 3)
        for r in heads:
            raw(g.at[1, 0, r], r).start()
        for peer in (near, across):
            pl.semaphore_signal(hsem.at[0], inc=1, device_id=peer, device_id_type=MESH)

    @pl.when(late == 1)
    def _():
        pl.semaphore_wait(barrier, 1)
        raw(g_hbm.at[1, 0, 0, heads[0]], heads[0]).start()
        for k in (1, 0):
            fetch_raw(k).start()
        fetch_raw(1).wait()
        raw(g.at[1, 0, heads[1]], heads[1]).start()
        fetch_rest()
        fetch_raw(0).wait()

    def meet():
        @pl.when(late == 0)
        def _():
            pl.semaphore_wait(hsem.at[0], 2)
            pl.semaphore_signal(hsem.at[1], inc=1, device_id=far, device_id_type=MESH)

        @pl.when(late == 1)
        def _():
            pl.semaphore_wait(hsem.at[1], 1)

    def momentum_one(i):
        if i == 0:
            fetch_momentum().wait()
            fetch_first().wait()
        if i == 1:
            fetch_others().wait()

        def body(r):
            grad = g[0, i, r].astype(F32)
            new = (BETA * m[i, r].astype(F32) + grad).astype(BF16)
            mn1[i, r] = new
            n[i, r] = (grad + BETA * new.astype(F32)).astype(BF16)

        pieces(0, rows, body)
        if i == 0:
            meet()
            fetch_params().start()
        first(i).start()

    def momentum_two(i):
        first(i).wait_recv()

        def body(r):
            grad = g[1, i, r].astype(F32)
            cur = mean(mn1[i, r], rm1[i, r])
            if i == 0:
                m1[r] = cur
            new = (BETA * cur.astype(F32) + grad).astype(BF16)
            mn2[i, r] = new
            n[mats + i, r] = (grad + BETA * new.astype(F32)).astype(BF16)

        pieces(0, rows, body)
        if i > 0:
            second(i).start()
        else:
            by_core(lambda own, other: share_m(own).start())

    for i in range(mats + 1):
        if i < mats:
            momentum_one(i)
        if i > 0:
            momentum_two(i - 1)

    def gram_part(slot):
        left, low_part = n[slot, :, :half], n[slot, :, half:]
        dims = (((0,), (0,)), ((), ()))
        gs[slot, :, :cols] = lax.dot_general(left, n[slot], dims, preferred_element_type=F32).astype(BF16)
        gs[slot, :, cols:] = lax.dot_general(low_part, low_part, dims, preferred_element_type=F32).astype(BF16)
        blocks(slot).start()

    each(STEPS * mats, gram_part)
    fetch_params().wait()

    def polys(slot):
        blocks(slot).wait_recv()
        top = gs[slot, :, :cols].astype(F32) + gr[slot, :, :cols].astype(F32)
        end = gs[slot, :, cols:].astype(F32) + gr[slot, :, cols:].astype(F32)
        eye = lax.broadcasted_iota(jnp.int32, (half, half), 0) == lax.broadcasted_iota(jnp.int32, (half, half), 1)
        trace = jnp.sum(jnp.where(eye, top[:, :half] + end, 0.0), keepdims=True)
        scale = 1.0 / (jnp.sqrt(trace) + 1e-07)
        square = scale * scale
        gram[:half, :] = top * square
        gram[half:, half:] = end * square
        gram[half:, :half] = (top[:, half:] * square).T
        low[...] = gram[...].astype(BF16)
        for it in range(NS_ITERS):
            def make_poly(t):
                r = pl.ds(pl.multiple_of(t * half, half), half)
                poly[it, r] = (COEF_B * low[r].astype(F32) + COEF_C * dot(low[r], low[...])).astype(BF16)

            def make_right(t):
                r = pl.ds(pl.multiple_of(t * half, half), half)
                value = COEF_A * gram[r] + dot(low[r], poly[it])
                right[r] = value
                rlow[r] = value.astype(BF16)

            def make_gram(t):
                r = pl.ds(pl.multiple_of(t * half, half), half)
                value = COEF_A * right[r] + dot(poly[it, r], rlow[...])
                gram[r] = value
                low[r] = value.astype(BF16)

            each(2, make_poly)
            if it < NS_ITERS - 1:
                each(2, make_right)
                each(2, make_gram)
        return scale

    def update(slot, r, scale):
        ycur = (n[slot, r].astype(F32) * scale).astype(BF16)
        for it in range(NS_ITERS):
            ycur = COEF_A * ycur.astype(F32) + dot(ycur, poly[it])
            if it < NS_ITERS - 1:
                ycur = ycur.astype(BF16)
        return ycur

    def step_one(i):
        scale = polys(i)

        def body(c):
            r = part(c)
            l1[i, r] = (p[i, r].astype(F32) - step_scale * update(i, r, scale)).astype(BF16)
            third(i, r).start()

        each(per, body)

    each(mats, step_one)

    third(pl.ds(0, mats), everything).wait_recv()

    def pair_mean(r):
        p1[r] = mean(l1[0, r], rl1[0, r])

    pieces(0, rows, pair_mean)
    by_core(lambda own, other: share_p(own).start())

    def step_two(i):
        scale = polys(mats + i)

        def body(c):
            r = part(c)
            cur = mean(l1[i, r], rl1[i, r]).astype(F32)
            l2[i, r] = (cur - step_scale * update(mats + i, r, scale)).astype(BF16)
            fourth(i, r, i * (1 - c // (per - 1)) if i == mats - 1 else i).start()

        each(per, body)

    for i in range(1, mats):
        step_two(i)

    def join(share, hand):
        def body(own, other):
            share(own).wait_recv()
            hand(own).start()
            hand(other).wait_recv()

        by_core(body)

    raw(g.at[1, 0], everything).wait_recv()
    join(share_m, pass_m)

    def momentum_far(r):
        grad = gb[r].astype(F32)
        new = (BETA * m1b[r].astype(F32) + grad).astype(BF16)
        n[spare, r] = (grad + BETA * new.astype(F32)).astype(BF16)
        m_out[0, 0, r] = mean(mn2[0, r], new)

    pieces(0, rows, momentum_far)
    gram_part(spare)

    own_scale = polys(mats)

    def own(c):
        r = part(c)
        l2[0, r] = (p1[r].astype(F32) - step_scale * update(mats, r, own_scale)).astype(BF16)

    each(per, own)

    far_scale = polys(spare)
    join(share_p, pass_p)

    def theirs(c):
        r = part(c)
        local = (p1b[r].astype(F32) - step_scale * update(spare, r, far_scale)).astype(BF16)
        p_out[0, 0, r] = mean(l2[0, r], local)

    each(per, theirs)

    second(others).wait_recv()
    for i in range(1, mats):
        def momentum_out(r):
            m_out[0, i, r] = mean(mn2[i, r], rm2[i, r])

        pieces(0, rows, momentum_out)

    def sent(ref, sem, peer):
        return send(ref, ref, sem, usem.at[0], peer)

    sent(n.at[pl.ds(0, STEPS * mats)], osem.at[1], near).wait_send()
    by_core(lambda own, other: [hand(own).wait_send() for hand in (pass_m, pass_p)])
    sent(gs, osem.at[2], across).wait_send()

    for i in range(1, mats):
        ends = [(0, rows - chunk, i), (rows - chunk, chunk, 0)] if i == mats - 1 else [(0, rows, i)]
        for start, size, at in ends:
            fourth(i, pl.ds(start, size), at).wait_recv()

            def params_out(r):
                p_out[0, i, r] = mean(l2[i, r], rl2[i, r])

            if at > 0:
                pieces(start, size, params_out)
    sent(n.at[pl.ds(0, STEPS * mats - 1)], osem.at[0], far).wait_send()
    by_core(lambda own, other: [share(own).wait_send() for share in (share_m, share_p)])


def put(chunk, p, m, own, got, p_out, m_out, last, sem):
    mats, rows, _ = own.shape
    start = rows - chunk
    moves = [
        (m, m_out),
        (p.at[0, pl.ds(0, mats - 1)], p_out.at[0, pl.ds(0, mats - 1)]),
        (p.at[0, mats - 1, pl.ds(0, start)], p_out.at[0, mats - 1, pl.ds(0, start)]),
        (last, p_out.at[0, mats - 1, pl.ds(start, chunk)]),
    ]
    copies = [pltpu.make_async_copy(src, dst, sem.at[k]) for k, (src, dst) in enumerate(moves)]
    for copy in copies[:-1]:
        copy.start()

    def body(k, c):
        r = pl.ds(pl.multiple_of(k * SUB, SUB), SUB)
        f = pl.ds(pl.multiple_of(start + k * SUB, SUB), SUB)
        last[r] = mean(own[mats - 1, f], got[mats - 1, f])
        return c

    lax.fori_loop(0, chunk // SUB, body, 0)
    copies[-1].start()
    for copy in copies:
        copy.wait()


def fused(params, momentum, grads):
    _, mats, rows, cols = params.shape
    chunk = min(CHUNK, rows // 2)
    whole, one = pltpu.VMEM((mats, rows, cols), BF16), pltpu.VMEM((rows, cols), BF16)
    slots = STEPS * mats + 1
    pack = pltpu.VMEM((slots, cols // 2, cols + cols // 2), BF16)
    small, small_low = pltpu.VMEM((cols, cols), F32), pltpu.VMEM((cols, cols), BF16)
    dma = pltpu.SemaphoreType.DMA
    anywhere = pl.BlockSpec(memory_space=pl.ANY)
    results = pl.pallas_call(
        functools.partial(kernel, chunk),
        out_shape=[pltpu.VMEM(params.shape, BF16)] * 2 + [pltpu.VMEM((mats, rows, cols), BF16)] * 2,
        in_specs=[anywhere] * 3,
        out_specs=[pl.BlockSpec(memory_space=pltpu.VMEM)] * 4,
        scratch_shapes=[
            whole, whole, pltpu.VMEM((STEPS, mats, rows, cols), BF16),
            whole, whole, whole, whole, pltpu.VMEM((slots, rows, cols), BF16),
            whole, whole, one, one, one, one, one, pack, pack,
            small, small_low, pltpu.VMEM((NS_ITERS, cols, cols), BF16), small, small_low,
            dma((5,)), dma((mats,)), dma((2,)), dma((1,)), dma((mats,)), dma((slots,)), dma((4,)), dma((3,)),
            pltpu.SemaphoreType.REGULAR((2,)),
        ],
        compiler_params=pltpu.CompilerParams(
            collective_id=0, has_side_effects=True, vmem_limit_bytes=50 * 2**20),
    )(params, momentum, grads)
    return pl.pallas_call(
        functools.partial(put, chunk),
        out_shape=[jax.ShapeDtypeStruct(params.shape, BF16)] * 2,
        in_specs=[pl.BlockSpec(memory_space=pltpu.VMEM)] * 4,
        out_specs=[anywhere] * 2,
        scratch_shapes=[pltpu.VMEM((chunk, cols), BF16), dma((4,))],
        compiler_params=pltpu.CompilerParams(vmem_limit_bytes=2 * 2**20),
    )(*[pltpu.with_memory_space_constraint(r, pltpu.VMEM) for r in results])


def solution(mesh):
    def program(params, momentum, grads):
        paired = mesh.shape["fsdp"] == 2 and params.shape[1] > 1
        return (fused if paired else shards)(params, momentum, grads)

    return jax.shard_map(
        program,
        mesh=mesh,
        in_specs=(
            P("replica", None, "fsdp", None),
            P("replica", None, "fsdp", None),
            P(None, "replica", None, "fsdp", None),
        ),
        out_specs=(P("replica", None, "fsdp", None), P("replica", None, "fsdp", None)),
        check_vma=False,
    )
```

```python
import functools
import math

import jax
import jax.numpy as jnp
from jax import lax
from jax.experimental import pallas as pl
from jax.experimental.pallas import tpu as pltpu
from jax.sharding import PartitionSpec as P

ROWS = 2048
COLS = 512
NS_ITERS = 3
STEPS = 2


BETA = 0.95
LEARN = 0.5
COEF_A = 3.4445
COEF_B = -4.775
COEF_C = 2.0315

MESH = pl.DeviceIdType.MESH
BF16 = jnp.bfloat16
F32 = jnp.float32


def partner(value, axis, apart):
    mask = 2**apart
    pairs = [(source, source ^ mask) for source in range(lax.axis_size(axis))]
    return lax.ppermute(value, axis, pairs)


def dot(a, b):
    return jnp.dot(a, b, preferred_element_type=F32)


def reduce_gram(nest):
    part = lax.dot_general(nest, nest, (((0,), (0,)), ((), ())), preferred_element_type=F32)
    half = part.shape[0] // 2
    packed = jnp.concatenate([part[:half], part[half:, half:]], axis=1).astype(BF16)
    if lax.axis_size("fsdp") == 2:
        whole = packed.astype(F32) + partner(packed, "fsdp", 0).astype(F32)
    else:
        whole = lax.psum(packed.astype(F32), "fsdp")
    top, low = whole[:, : 2 * half], whole[:, 2 * half :]
    return jnp.concatenate([top, jnp.concatenate([top[:, half:].T, low], axis=1)], axis=0)


def orthogonalize(nest, gram):
    scale = 1.0 / (jnp.sqrt(jnp.trace(gram)) + 1e-07)
    gram = gram * (scale * scale)
    ycur = (nest.astype(F32) * scale).astype(BF16)
    for it in range(NS_ITERS):
        low = gram.astype(BF16)
        poly = (COEF_B * low.astype(F32) + COEF_C * dot(low, low)).astype(BF16)
        if it < NS_ITERS - 1:
            right = COEF_A * gram + dot(low, poly)
            gram = COEF_A * right + dot(poly, right.astype(BF16))
        ycur = COEF_A * ycur.astype(F32) + dot(ycur, poly)
        if it < NS_ITERS - 1:
            ycur = ycur.astype(BF16)
    return ycur


def mean(a, b):
    return (0.5 * (a.astype(F32) + b.astype(F32))).astype(BF16)


def shards(params, momentum, grads):
    mats = params.shape[1]
    step_scale = LEARN * 0.2 * math.sqrt(max(ROWS, COLS))
    nests = []
    mcur = [momentum[0, i] for i in range(mats)]
    for step in range(STEPS):
        grad = [grads[step, 0, i].astype(F32) for i in range(mats)]
        m_new = [(BETA * m.astype(F32) + g).astype(BF16) for m, g in zip(mcur, grad)]
        nests.append([(g + BETA * m.astype(F32)).astype(BF16) for m, g in zip(m_new, grad)])
        mcur = [mean(m, partner(m, "replica", step)) for m in m_new]
    grams = [[reduce_gram(n) for n in row] for row in nests]
    pcur = [params[0, i] for i in range(mats)]
    for step in range(STEPS):
        for i in range(mats):
            update = orthogonalize(nests[step][i], grams[step][i])
            local = (pcur[i].astype(F32) - step_scale * update).astype(BF16)
            pcur[i] = mean(local, partner(local, "replica", step))
    return (jnp.stack(pcur)[None], jnp.stack(mcur)[None])


SUB = 64
HEAD = 128
SKEW = 48
CHUNK = 128


def kernel(chunk, p_hbm, m_hbm, g_hbm, p_out, m_out,
           p, m, g, mn1, rm1, mn2, rm2, n, l1, rl1, l2, rl2,
           m1, m1b, p1, p1b, gb, gs, gr, gram, low, poly, right, rlow,
           isem, msem, esem, lsem, usem, bsem, wsem, osem, hsem):
    mats, rows, cols = p.shape
    half = cols // 2
    per = rows // chunk
    spare = STEPS * mats
    step_scale = LEARN * 0.2 * math.sqrt(max(ROWS, COLS))
    side = lax.axis_index("fsdp")
    rep = lax.axis_index("replica")
    core = rep % 2
    late = (rep // 2) % 2
    across = {"fsdp": 1 - side}
    near = {"replica": rep + 1 - 2 * core}
    far = {"replica": rep + 2 - 4 * late}
    cut = rows // 2 - SKEW
    parts = [pl.ds(0, cut), pl.ds(cut, rows - cut)]
    others = pl.ds(1, mats - 1)

    def each(total, body):
        lax.fori_loop(0, total, lambda k, c: (body(k), c)[1], 0)

    def part(c):
        return pl.ds(pl.multiple_of(c * chunk, chunk), chunk)

    everything = pl.ds(0, rows)

    def pieces(start, size, body):
        each(size // SUB, lambda k: body(pl.ds(pl.multiple_of(start + k * SUB, SUB), SUB)))

    def mean(a, b):
        return (0.5 * (a.astype(F32) + b.astype(F32))).astype(BF16)

    heads = [pl.ds(0, HEAD), pl.ds(HEAD, rows - HEAD)]

    def fetch_raw(k):
        return pltpu.make_async_copy(g_hbm.at[1, 0, 0, heads[k]], g.at[1, 0, heads[k]], isem.at[k])

    def fetch_momentum():
        return pltpu.make_async_copy(m_hbm.at[0], m, isem.at[2])

    def fetch_params():
        return pltpu.make_async_copy(p_hbm.at[0], p, isem.at[2])

    def fetch_first():
        return pltpu.make_async_copy(g_hbm.at[0, 0, 0], g.at[0, 0], isem.at[3])

    def fetch_others():
        return pltpu.make_async_copy(g_hbm.at[:, 0, others], g.at[:, others], isem.at[4])

    def send(src, dst, sent, got, peer):
        return pltpu.make_async_remote_copy(
            src_ref=src, dst_ref=dst, send_sem=sent, recv_sem=got, device_id=peer, device_id_type=MESH)

    def raw(src, r):
        return send(src, gb.at[r], osem.at[0], wsem.at[0], far)

    def first(i):
        return send(mn1.at[i], rm1.at[i], osem.at[1], msem.at[i], near)

    def second(i):
        return send(mn2.at[i], rm2.at[i], osem.at[0], wsem.at[1], far)

    def by_core(body):
        for c in range(2):
            @pl.when(core == c)
            def _(c=c):
                body(parts[c], parts[1 - c])

    def share_m(r):
        return send(m1.at[r], m1b.at[r], osem.at[0], wsem.at[2], far)

    def pass_m(r):
        return send(m1b.at[r], m1b.at[r], osem.at[1], esem.at[0], near)

    def third(i, r):
        return send(l1.at[i, r], rl1.at[i, r], osem.at[1], lsem.at[0], near)

    def share_p(r):
        return send(p1.at[r], p1b.at[r], osem.at[0], wsem.at[3], far)

    def pass_p(r):
        return send(p1b.at[r], p1b.at[r], osem.at[1], esem.at[1], near)

    def fourth(i, r, at):
        return send(l2.at[i, r], rl2.at[i, r], osem.at[0], usem.at[at], far)

    def blocks(slot):
        return send(gs.at[slot], gr.at[slot], osem.at[2], bsem.at[slot], across)

    barrier = pltpu.get_barrier_semaphore()
    pl.semaphore_signal(barrier, inc=1, device_id=far, device_id_type=MESH)

    @pl.when(late == 0)
    def _():
        for peer in (near, across):
            pl.semaphore_signal(barrier, inc=1, device_id=peer, device_id_type=MESH)

    def fetch_rest():
        fetch_momentum().start()
        fetch_first().start()
        fetch_others().start()

    @pl.when(late == 0)
    def _():
        for k in range(2):
            fetch_raw(k).start()
        fetch_rest()
        for k in range(2):
            fetch_raw(k).wait()
        pl.semaphore_wait(barrier, 3)
        for r in heads:
            raw(g.at[1, 0, r], r).start()
        for peer in (near, across):
            pl.semaphore_signal(hsem.at[0], inc=1, device_id=peer, device_id_type=MESH)

    @pl.when(late == 1)
    def _():
        pl.semaphore_wait(barrier, 1)
        raw(g_hbm.at[1, 0, 0, heads[0]], heads[0]).start()
        for k in (1, 0):
            fetch_raw(k).start()
        fetch_raw(1).wait()
        raw(g.at[1, 0, heads[1]], heads[1]).start()
        fetch_rest()
        fetch_raw(0).wait()

    def meet():
        @pl.when(late == 0)
        def _():
            pl.semaphore_wait(hsem.at[0], 2)
            pl.semaphore_signal(hsem.at[1], inc=1, device_id=far, device_id_type=MESH)

        @pl.when(late == 1)
        def _():
            pl.semaphore_wait(hsem.at[1], 1)

    def momentum_one(i):
        if i == 0:
            fetch_momentum().wait()
            fetch_first().wait()
        if i == 1:
            fetch_others().wait()

        def body(r):
            grad = g[0, i, r].astype(F32)
            new = (BETA * m[i, r].astype(F32) + grad).astype(BF16)
            mn1[i, r] = new
            n[i, r] = (grad + BETA * new.astype(F32)).astype(BF16)

        pieces(0, rows, body)
        if i == 0:
            meet()
            fetch_params().start()
        first(i).start()

    def momentum_two(i):
        first(i).wait_recv()

        def body(r):
            grad = g[1, i, r].astype(F32)
            cur = mean(mn1[i, r], rm1[i, r])
            if i == 0:
                m1[r] = cur
            new = (BETA * cur.astype(F32) + grad).astype(BF16)
            mn2[i, r] = new
            n[mats + i, r] = (grad + BETA * new.astype(F32)).astype(BF16)

        pieces(0, rows, body)
        if i > 0:
            second(i).start()
        else:
            by_core(lambda own, other: share_m(own).start())

    for i in range(mats + 1):
        if i < mats:
            momentum_one(i)
        if i > 0:
            momentum_two(i - 1)

    def gram_part(slot):
        left, low_part = n[slot, :, :half], n[slot, :, half:]
        dims = (((0,), (0,)), ((), ()))
        gs[slot, :, :cols] = lax.dot_general(left, n[slot], dims, preferred_element_type=F32).astype(BF16)
        gs[slot, :, cols:] = lax.dot_general(low_part, low_part, dims, preferred_element_type=F32).astype(BF16)
        blocks(slot).start()

    each(STEPS * mats, gram_part)
    fetch_params().wait()

    def polys(slot):
        blocks(slot).wait_recv()
        top = gs[slot, :, :cols].astype(F32) + gr[slot, :, :cols].astype(F32)
        end = gs[slot, :, cols:].astype(F32) + gr[slot, :, cols:].astype(F32)
        eye = lax.broadcasted_iota(jnp.int32, (half, half), 0) == lax.broadcasted_iota(jnp.int32, (half, half), 1)
        trace = jnp.sum(jnp.where(eye, top[:, :half] + end, 0.0), keepdims=True)
        scale = 1.0 / (jnp.sqrt(trace) + 1e-07)
        square = scale * scale
        gram[:half, :] = top * square
        gram[half:, half:] = end * square
        gram[half:, :half] = (top[:, half:] * square).T
        low[...] = gram[...].astype(BF16)
        for it in range(NS_ITERS):
            def make_poly(t):
                r = pl.ds(pl.multiple_of(t * half, half), half)
                poly[it, r] = (COEF_B * low[r].astype(F32) + COEF_C * dot(low[r], low[...])).astype(BF16)

            def make_right(t):
                r = pl.ds(pl.multiple_of(t * half, half), half)
                value = COEF_A * gram[r] + dot(low[r], poly[it])
                right[r] = value
                rlow[r] = value.astype(BF16)

            def make_gram(t):
                r = pl.ds(pl.multiple_of(t * half, half), half)
                value = COEF_A * right[r] + dot(poly[it, r], rlow[...])
                gram[r] = value
                low[r] = value.astype(BF16)

            each(2, make_poly)
            if it < NS_ITERS - 1:
                each(2, make_right)
                each(2, make_gram)
        return scale

    def update(slot, r, scale):
        ycur = (n[slot, r].astype(F32) * scale).astype(BF16)
        for it in range(NS_ITERS):
            ycur = COEF_A * ycur.astype(F32) + dot(ycur, poly[it])
            if it < NS_ITERS - 1:
                ycur = ycur.astype(BF16)
        return ycur

    def step_one(i):
        scale = polys(i)

        def body(c):
            r = part(c)
            l1[i, r] = (p[i, r].astype(F32) - step_scale * update(i, r, scale)).astype(BF16)
            third(i, r).start()

        each(per, body)

    each(mats, step_one)

    third(pl.ds(0, mats), everything).wait_recv()

    def pair_mean(r):
        p1[r] = mean(l1[0, r], rl1[0, r])

    pieces(0, rows, pair_mean)
    by_core(lambda own, other: share_p(own).start())

    def step_two(i):
        scale = polys(mats + i)

        def body(c):
            r = part(c)
            cur = mean(l1[i, r], rl1[i, r]).astype(F32)
            l2[i, r] = (cur - step_scale * update(mats + i, r, scale)).astype(BF16)
            fourth(i, r, i * (1 - c // (per - 1)) if i == mats - 1 else i).start()

        each(per, body)

    for i in range(1, mats):
        step_two(i)

    def join(share, hand):
        def body(own, other):
            share(own).wait_recv()
            hand(own).start()
            hand(other).wait_recv()

        by_core(body)

    raw(g.at[1, 0], everything).wait_recv()
    join(share_m, pass_m)

    def momentum_far(r):
        grad = gb[r].astype(F32)
        new = (BETA * m1b[r].astype(F32) + grad).astype(BF16)
        n[spare, r] = (grad + BETA * new.astype(F32)).astype(BF16)
        m_out[0, 0, r] = mean(mn2[0, r], new)

    pieces(0, rows, momentum_far)
    gram_part(spare)

    own_scale = polys(mats)

    def own(c):
        r = part(c)
        l2[0, r] = (p1[r].astype(F32) - step_scale * update(mats, r, own_scale)).astype(BF16)

    each(per, own)

    far_scale = polys(spare)
    join(share_p, pass_p)

    def theirs(c):
        r = part(c)
        local = (p1b[r].astype(F32) - step_scale * update(spare, r, far_scale)).astype(BF16)
        p_out[0, 0, r] = mean(l2[0, r], local)

    each(per, theirs)

    second(others).wait_recv()
    for i in range(1, mats):
        def momentum_out(r):
            m_out[0, i, r] = mean(mn2[i, r], rm2[i, r])

        pieces(0, rows, momentum_out)

    def sent(ref, sem, peer):
        return send(ref, ref, sem, usem.at[0], peer)

    sent(n.at[pl.ds(0, STEPS * mats)], osem.at[1], near).wait_send()
    by_core(lambda own, other: [hand(own).wait_send() for hand in (pass_m, pass_p)])
    sent(gs, osem.at[2], across).wait_send()

    for i in range(1, mats):
        ends = [(0, rows - chunk, i), (rows - chunk, chunk, 0)] if i == mats - 1 else [(0, rows, i)]
        for start, size, at in ends:
            fourth(i, pl.ds(start, size), at).wait_recv()

            def params_out(r):
                p_out[0, i, r] = mean(l2[i, r], rl2[i, r])

            pieces(start, size, params_out)
    sent(n.at[pl.ds(0, STEPS * mats - 1)], osem.at[0], far).wait_send()
    by_core(lambda own, other: [share(own).wait_send() for share in (share_m, share_p)])


def put(p, m, p_out, m_out, sem):
    copies = [pltpu.make_async_copy(src, dst, sem.at[k]) for k, (src, dst) in enumerate(((p, p_out), (m, m_out)))]
    for copy in copies:
        copy.start()
    for copy in copies:
        copy.wait()


def fused(params, momentum, grads):
    _, mats, rows, cols = params.shape
    chunk = min(CHUNK, rows // 2)
    whole, one = pltpu.VMEM((mats, rows, cols), BF16), pltpu.VMEM((rows, cols), BF16)
    slots = STEPS * mats + 1
    pack = pltpu.VMEM((slots, cols // 2, cols + cols // 2), BF16)
    small, small_low = pltpu.VMEM((cols, cols), F32), pltpu.VMEM((cols, cols), BF16)
    dma = pltpu.SemaphoreType.DMA
    anywhere = pl.BlockSpec(memory_space=pl.ANY)
    results = pl.pallas_call(
        functools.partial(kernel, chunk),
        out_shape=[pltpu.VMEM(params.shape, BF16)] * 2,
        in_specs=[anywhere] * 3,
        out_specs=[pl.BlockSpec(memory_space=pltpu.VMEM)] * 2,
        scratch_shapes=[
            whole, whole, pltpu.VMEM((STEPS, mats, rows, cols), BF16),
            whole, whole, whole, whole, pltpu.VMEM((slots, rows, cols), BF16),
            whole, whole, whole, whole, one, one, one, one, one, pack, pack,
            small, small_low, pltpu.VMEM((NS_ITERS, cols, cols), BF16), small, small_low,
            dma((5,)), dma((mats,)), dma((2,)), dma((1,)), dma((mats,)), dma((slots,)), dma((4,)), dma((3,)),
            pltpu.SemaphoreType.REGULAR((2,)),
        ],
        compiler_params=pltpu.CompilerParams(
            collective_id=0, has_side_effects=True, vmem_limit_bytes=59 * 2**20),
    )(params, momentum, grads)
    return pl.pallas_call(
        put,
        out_shape=[jax.ShapeDtypeStruct(params.shape, BF16)] * 2,
        in_specs=[pl.BlockSpec(memory_space=pltpu.VMEM)] * 2,
        out_specs=[anywhere] * 2,
        scratch_shapes=[dma((2,))],
        compiler_params=pltpu.CompilerParams(vmem_limit_bytes=2**20),
    )(*[pltpu.with_memory_space_constraint(r, pltpu.VMEM) for r in results])


def solution(mesh):
    def program(params, momentum, grads):
        paired = mesh.shape["fsdp"] == 2 and params.shape[1] > 1
        return (fused if paired else shards)(params, momentum, grads)

    return jax.shard_map(
        program,
        mesh=mesh,
        in_specs=(
            P("replica", None, "fsdp", None),
            P("replica", None, "fsdp", None),
            P(None, "replica", None, "fsdp", None),
        ),
        out_specs=(P("replica", None, "fsdp", None), P("replica", None, "fsdp", None)),
        check_vma=False,
    )
```

```python
import functools
import math

import jax
import jax.numpy as jnp
from jax import lax
from jax.experimental import pallas as pl
from jax.experimental.pallas import tpu as pltpu
from jax.sharding import PartitionSpec as P

ROWS = 2048
COLS = 512
NS_ITERS = 3
STEPS = 2


BETA = 0.95
LEARN = 0.5
COEF_A = 3.4445
COEF_B = -4.775
COEF_C = 2.0315

MESH = pl.DeviceIdType.MESH
BF16 = jnp.bfloat16
F32 = jnp.float32


def partner(value, axis, apart):
    mask = 2**apart
    pairs = [(source, source ^ mask) for source in range(lax.axis_size(axis))]
    return lax.ppermute(value, axis, pairs)


def dot(a, b):
    return jnp.dot(a, b, preferred_element_type=F32)


def reduce_gram(nest):
    part = lax.dot_general(nest, nest, (((0,), (0,)), ((), ())), preferred_element_type=F32)
    half = part.shape[0] // 2
    packed = jnp.concatenate([part[:half], part[half:, half:]], axis=1).astype(BF16)
    if lax.axis_size("fsdp") == 2:
        whole = packed.astype(F32) + partner(packed, "fsdp", 0).astype(F32)
    else:
        whole = lax.psum(packed.astype(F32), "fsdp")
    top, low = whole[:, : 2 * half], whole[:, 2 * half :]
    return jnp.concatenate([top, jnp.concatenate([top[:, half:].T, low], axis=1)], axis=0)


def orthogonalize(nest, gram):
    scale = 1.0 / (jnp.sqrt(jnp.trace(gram)) + 1e-07)
    gram = gram * (scale * scale)
    ycur = (nest.astype(F32) * scale).astype(BF16)
    for it in range(NS_ITERS):
        low = gram.astype(BF16)
        poly = (COEF_B * low.astype(F32) + COEF_C * dot(low, low)).astype(BF16)
        if it < NS_ITERS - 1:
            right = COEF_A * gram + dot(low, poly)
            gram = COEF_A * right + dot(poly, right.astype(BF16))
        ycur = COEF_A * ycur.astype(F32) + dot(ycur, poly)
        if it < NS_ITERS - 1:
            ycur = ycur.astype(BF16)
    return ycur


def mean(a, b):
    return (0.5 * (a.astype(F32) + b.astype(F32))).astype(BF16)


def shards(params, momentum, grads):
    mats = params.shape[1]
    step_scale = LEARN * 0.2 * math.sqrt(max(ROWS, COLS))
    nests = []
    mcur = [momentum[0, i] for i in range(mats)]
    for step in range(STEPS):
        grad = [grads[step, 0, i].astype(F32) for i in range(mats)]
        m_new = [(BETA * m.astype(F32) + g).astype(BF16) for m, g in zip(mcur, grad)]
        nests.append([(g + BETA * m.astype(F32)).astype(BF16) for m, g in zip(m_new, grad)])
        mcur = [mean(m, partner(m, "replica", step)) for m in m_new]
    grams = [[reduce_gram(n) for n in row] for row in nests]
    pcur = [params[0, i] for i in range(mats)]
    for step in range(STEPS):
        for i in range(mats):
            update = orthogonalize(nests[step][i], grams[step][i])
            local = (pcur[i].astype(F32) - step_scale * update).astype(BF16)
            pcur[i] = mean(local, partner(local, "replica", step))
    return (jnp.stack(pcur)[None], jnp.stack(mcur)[None])


SUB = 64
HEAD = 128
SKEW = 32
CHUNK = 256


def kernel(chunk, p_hbm, m_hbm, g_hbm, p_out, m_out,
           p, m, g, mn1, rm1, mn2, rm2, n, l1, rl1, l2, rl2,
           m1, m1b, p1, p1b, gb, gs, gr, gram, low, poly, right, rlow,
           isem, msem, esem, lsem, usem, bsem, wsem, osem, hsem):
    mats, rows, cols = p.shape
    half = cols // 2
    per = rows // chunk
    spare = STEPS * mats
    step_scale = LEARN * 0.2 * math.sqrt(max(ROWS, COLS))
    side = lax.axis_index("fsdp")
    rep = lax.axis_index("replica")
    core = rep % 2
    late = (rep // 2) % 2
    across = {"fsdp": 1 - side}
    near = {"replica": rep + 1 - 2 * core}
    far = {"replica": rep + 2 - 4 * late}
    cut = rows // 2 - SKEW
    parts = [pl.ds(0, cut), pl.ds(cut, rows - cut)]
    others = pl.ds(1, mats - 1)

    def each(total, body):
        lax.fori_loop(0, total, lambda k, c: (body(k), c)[1], 0)

    def part(c):
        return pl.ds(pl.multiple_of(c * chunk, chunk), chunk)

    everything = pl.ds(0, rows)

    def pieces(start, size, body):
        each(size // SUB, lambda k: body(pl.ds(pl.multiple_of(start + k * SUB, SUB), SUB)))

    def mean(a, b):
        return (0.5 * (a.astype(F32) + b.astype(F32))).astype(BF16)

    heads = [pl.ds(0, HEAD), pl.ds(HEAD, rows - HEAD)]

    def fetch_raw(k):
        return pltpu.make_async_copy(g_hbm.at[1, 0, 0, heads[k]], g.at[1, 0, heads[k]], isem.at[k])

    def fetch_momentum():
        return pltpu.make_async_copy(m_hbm.at[0], m, isem.at[2])

    def fetch_params():
        return pltpu.make_async_copy(p_hbm.at[0], p, isem.at[2])

    def fetch_first():
        return pltpu.make_async_copy(g_hbm.at[0, 0, 0], g.at[0, 0], isem.at[3])

    def fetch_others():
        return pltpu.make_async_copy(g_hbm.at[:, 0, others], g.at[:, others], isem.at[4])

    def send(src, dst, sent, got, peer):
        return pltpu.make_async_remote_copy(
            src_ref=src, dst_ref=dst, send_sem=sent, recv_sem=got, device_id=peer, device_id_type=MESH)

    def raw(src, r):
        return send(src, gb.at[r], osem.at[0], wsem.at[0], far)

    def first(i):
        return send(mn1.at[i], rm1.at[i], osem.at[1], msem.at[i], near)

    def second(i):
        return send(mn2.at[i], rm2.at[i], osem.at[0], wsem.at[1], far)

    def by_core(body):
        for c in range(2):
            @pl.when(core == c)
            def _(c=c):
                body(parts[c], parts[1 - c])

    def share_m(r):
        return send(m1.at[r], m1b.at[r], osem.at[0], wsem.at[2], far)

    def pass_m(r):
        return send(m1b.at[r], m1b.at[r], osem.at[1], esem.at[0], near)

    def third(i, r):
        return send(l1.at[i, r], rl1.at[i, r], osem.at[1], lsem.at[0], near)

    def share_p(r):
        return send(p1.at[r], p1b.at[r], osem.at[0], wsem.at[3], far)

    def pass_p(r):
        return send(p1b.at[r], p1b.at[r], osem.at[1], esem.at[1], near)

    def fourth(i, r, at):
        return send(l2.at[i, r], rl2.at[i, r], osem.at[0], usem.at[at], far)

    def blocks(slot):
        return send(gs.at[slot], gr.at[slot], osem.at[2], bsem.at[slot], across)

    barrier = pltpu.get_barrier_semaphore()
    pl.semaphore_signal(barrier, inc=1, device_id=far, device_id_type=MESH)

    @pl.when(late == 0)
    def _():
        for peer in (near, across):
            pl.semaphore_signal(barrier, inc=1, device_id=peer, device_id_type=MESH)

    def fetch_rest():
        fetch_momentum().start()
        fetch_first().start()
        fetch_others().start()

    @pl.when(late == 0)
    def _():
        for k in range(2):
            fetch_raw(k).start()
        fetch_rest()
        for k in range(2):
            fetch_raw(k).wait()
        pl.semaphore_wait(barrier, 3)
        for r in heads:
            raw(g.at[1, 0, r], r).start()
        for peer in (near, across):
            pl.semaphore_signal(hsem.at[0], inc=1, device_id=peer, device_id_type=MESH)

    @pl.when(late == 1)
    def _():
        pl.semaphore_wait(barrier, 1)
        raw(g_hbm.at[1, 0, 0, heads[0]], heads[0]).start()
        for k in (1, 0):
            fetch_raw(k).start()
        fetch_raw(1).wait()
        raw(g.at[1, 0, heads[1]], heads[1]).start()
        fetch_rest()
        fetch_raw(0).wait()

    def meet():
        @pl.when(late == 0)
        def _():
            pl.semaphore_wait(hsem.at[0], 2)
            pl.semaphore_signal(hsem.at[1], inc=1, device_id=far, device_id_type=MESH)

        @pl.when(late == 1)
        def _():
            pl.semaphore_wait(hsem.at[1], 1)

    def momentum_one(i):
        if i == 0:
            fetch_momentum().wait()
            fetch_first().wait()
        if i == 1:
            fetch_others().wait()

        def body(r):
            grad = g[0, i, r].astype(F32)
            new = (BETA * m[i, r].astype(F32) + grad).astype(BF16)
            mn1[i, r] = new
            n[i, r] = (grad + BETA * new.astype(F32)).astype(BF16)

        pieces(0, rows, body)
        if i == 0:
            meet()
            fetch_params().start()
        first(i).start()

    def momentum_two(i):
        first(i).wait_recv()

        def body(r):
            grad = g[1, i, r].astype(F32)
            cur = mean(mn1[i, r], rm1[i, r])
            if i == 0:
                m1[r] = cur
            new = (BETA * cur.astype(F32) + grad).astype(BF16)
            mn2[i, r] = new
            n[mats + i, r] = (grad + BETA * new.astype(F32)).astype(BF16)

        pieces(0, rows, body)
        if i > 0:
            second(i).start()
        else:
            by_core(lambda own, other: share_m(own).start())

    for i in range(mats + 1):
        if i < mats:
            momentum_one(i)
        if i > 0:
            momentum_two(i - 1)

    def gram_part(slot):
        left, low_part = n[slot, :, :half], n[slot, :, half:]
        dims = (((0,), (0,)), ((), ()))
        gs[slot, :, :cols] = lax.dot_general(left, n[slot], dims, preferred_element_type=F32).astype(BF16)
        gs[slot, :, cols:] = lax.dot_general(low_part, low_part, dims, preferred_element_type=F32).astype(BF16)
        blocks(slot).start()

    each(STEPS * mats, gram_part)
    fetch_params().wait()

    def polys(slot):
        blocks(slot).wait_recv()
        top = gs[slot, :, :cols].astype(F32) + gr[slot, :, :cols].astype(F32)
        end = gs[slot, :, cols:].astype(F32) + gr[slot, :, cols:].astype(F32)
        eye = lax.broadcasted_iota(jnp.int32, (half, half), 0) == lax.broadcasted_iota(jnp.int32, (half, half), 1)
        trace = jnp.sum(jnp.where(eye, top[:, :half] + end, 0.0), keepdims=True)
        scale = 1.0 / (jnp.sqrt(trace) + 1e-07)
        square = scale * scale
        gram[:half, :] = top * square
        gram[half:, half:] = end * square
        gram[half:, :half] = (top[:, half:] * square).T
        low[...] = gram[...].astype(BF16)
        for it in range(NS_ITERS):
            def make_poly(t):
                r = pl.ds(pl.multiple_of(t * half, half), half)
                poly[it, r] = (COEF_B * low[r].astype(F32) + COEF_C * dot(low[r], low[...])).astype(BF16)

            def make_right(t):
                r = pl.ds(pl.multiple_of(t * half, half), half)
                value = COEF_A * gram[r] + dot(low[r], poly[it])
                right[r] = value
                rlow[r] = value.astype(BF16)

            def make_gram(t):
                r = pl.ds(pl.multiple_of(t * half, half), half)
                value = COEF_A * right[r] + dot(poly[it, r], rlow[...])
                gram[r] = value
                low[r] = value.astype(BF16)

            each(2, make_poly)
            if it < NS_ITERS - 1:
                each(2, make_right)
                each(2, make_gram)
        return scale

    def update(slot, r, scale):
        ycur = (n[slot, r].astype(F32) * scale).astype(BF16)
        for it in range(NS_ITERS):
            ycur = COEF_A * ycur.astype(F32) + dot(ycur, poly[it])
            if it < NS_ITERS - 1:
                ycur = ycur.astype(BF16)
        return ycur

    def step_one(i):
        scale = polys(i)

        def body(c):
            r = part(c)
            l1[i, r] = (p[i, r].astype(F32) - step_scale * update(i, r, scale)).astype(BF16)
            third(i, r).start()

        each(per, body)

    each(mats, step_one)

    third(pl.ds(0, mats), everything).wait_recv()

    def pair_mean(r):
        p1[r] = mean(l1[0, r], rl1[0, r])

    pieces(0, rows, pair_mean)
    by_core(lambda own, other: share_p(own).start())

    def step_two(i):
        scale = polys(mats + i)

        def body(c):
            r = part(c)
            cur = mean(l1[i, r], rl1[i, r]).astype(F32)
            l2[i, r] = (cur - step_scale * update(mats + i, r, scale)).astype(BF16)
            fourth(i, r, i * (1 - c // (per - 1)) if i == mats - 1 else i).start()

        each(per, body)

    for i in range(1, mats):
        step_two(i)

    def join(share, hand):
        def body(own, other):
            share(own).wait_recv()
            hand(own).start()
            hand(other).wait_recv()

        by_core(body)

    raw(g.at[1, 0], everything).wait_recv()
    join(share_m, pass_m)

    def momentum_far(r):
        grad = gb[r].astype(F32)
        new = (BETA * m1b[r].astype(F32) + grad).astype(BF16)
        n[spare, r] = (grad + BETA * new.astype(F32)).astype(BF16)
        m_out[0, 0, r] = mean(mn2[0, r], new)

    pieces(0, rows, momentum_far)
    gram_part(spare)

    own_scale = polys(mats)

    def own(c):
        r = part(c)
        l2[0, r] = (p1[r].astype(F32) - step_scale * update(mats, r, own_scale)).astype(BF16)

    each(per, own)

    far_scale = polys(spare)
    join(share_p, pass_p)

    def theirs(c):
        r = part(c)
        local = (p1b[r].astype(F32) - step_scale * update(spare, r, far_scale)).astype(BF16)
        p_out[0, 0, r] = mean(l2[0, r], local)

    each(per, theirs)

    second(others).wait_recv()
    for i in range(1, mats):
        def momentum_out(r):
            m_out[0, i, r] = mean(mn2[i, r], rm2[i, r])

        pieces(0, rows, momentum_out)

    def sent(ref, sem, peer):
        return send(ref, ref, sem, usem.at[0], peer)

    sent(n.at[pl.ds(0, STEPS * mats)], osem.at[1], near).wait_send()
    by_core(lambda own, other: [hand(own).wait_send() for hand in (pass_m, pass_p)])
    sent(gs, osem.at[2], across).wait_send()

    for i in range(1, mats):
        ends = [(0, rows - chunk, i), (rows - chunk, chunk, 0)] if i == mats - 1 else [(0, rows, i)]
        for start, size, at in ends:
            fourth(i, pl.ds(start, size), at).wait_recv()

            def params_out(r):
                p_out[0, i, r] = mean(l2[i, r], rl2[i, r])

            pieces(start, size, params_out)
    sent(n.at[pl.ds(0, STEPS * mats - 1)], osem.at[0], far).wait_send()
    by_core(lambda own, other: [share(own).wait_send() for share in (share_m, share_p)])


def put(p, m, p_out, m_out, sem):
    copies = [pltpu.make_async_copy(src, dst, sem.at[k]) for k, (src, dst) in enumerate(((p, p_out), (m, m_out)))]
    for copy in copies:
        copy.start()
    for copy in copies:
        copy.wait()


def fused(params, momentum, grads):
    _, mats, rows, cols = params.shape
    chunk = min(CHUNK, rows // 2)
    whole, one = pltpu.VMEM((mats, rows, cols), BF16), pltpu.VMEM((rows, cols), BF16)
    slots = STEPS * mats + 1
    pack = pltpu.VMEM((slots, cols // 2, cols + cols // 2), BF16)
    small, small_low = pltpu.VMEM((cols, cols), F32), pltpu.VMEM((cols, cols), BF16)
    dma = pltpu.SemaphoreType.DMA
    anywhere = pl.BlockSpec(memory_space=pl.ANY)
    results = pl.pallas_call(
        functools.partial(kernel, chunk),
        out_shape=[pltpu.VMEM(params.shape, BF16)] * 2,
        in_specs=[anywhere] * 3,
        out_specs=[pl.BlockSpec(memory_space=pltpu.VMEM)] * 2,
        scratch_shapes=[
            whole, whole, pltpu.VMEM((STEPS, mats, rows, cols), BF16),
            whole, whole, whole, whole, pltpu.VMEM((slots, rows, cols), BF16),
            whole, whole, whole, whole, one, one, one, one, one, pack, pack,
            small, small_low, pltpu.VMEM((NS_ITERS, cols, cols), BF16), small, small_low,
            dma((5,)), dma((mats,)), dma((2,)), dma((1,)), dma((mats,)), dma((slots,)), dma((4,)), dma((3,)),
            pltpu.SemaphoreType.REGULAR((2,)),
        ],
        compiler_params=pltpu.CompilerParams(
            collective_id=0, has_side_effects=True, vmem_limit_bytes=59 * 2**20),
    )(params, momentum, grads)
    return pl.pallas_call(
        put,
        out_shape=[jax.ShapeDtypeStruct(params.shape, BF16)] * 2,
        in_specs=[pl.BlockSpec(memory_space=pltpu.VMEM)] * 2,
        out_specs=[anywhere] * 2,
        scratch_shapes=[dma((2,))],
        compiler_params=pltpu.CompilerParams(vmem_limit_bytes=2**20),
    )(*[pltpu.with_memory_space_constraint(r, pltpu.VMEM) for r in results])


def solution(mesh):
    def program(params, momentum, grads):
        paired = mesh.shape["fsdp"] == 2 and params.shape[1] > 1
        return (fused if paired else shards)(params, momentum, grads)

    return jax.shard_map(
        program,
        mesh=mesh,
        in_specs=(
            P("replica", None, "fsdp", None),
            P("replica", None, "fsdp", None),
            P(None, "replica", None, "fsdp", None),
        ),
        out_specs=(P("replica", None, "fsdp", None), P("replica", None, "fsdp", None)),
        check_vma=False,
    )
```
